32 devices in a mesh: tx: 8 (over z, x), ty: 4 (over y, core).
Axes of the slice: x: 2, y: 2, z: 4, core: 2. Of those that a mesh axis runs over, the one named last changes fastest.
Arguments:
- probes: bfloat16 [8, 64, 64, 128], P('tx', 'ty'), may hold values from -6 to 6
- left_probes: bfloat16 [8, 64, 64, 128], P('tx', 'ty'), may hold values from -6 to 6
- angles: float32 [8, 64, 64], P('tx', 'ty'), may hold values from -3.140625 to 3.140625
- cluster_hopping: bfloat16 [8, 64, 128, 128], P('tx', 'ty'), may hold values from -0.0625 to 0.0625
- east_bonds: bfloat16 [8, 64, 128, 128], P('tx', 'ty'), may hold values from -0.046875 to 0.046875
- south_bonds: bfloat16 [8, 64, 128, 128], P('tx', 'ty'), may hold values from -0.046875 to 0.046875
- bond_mask: int32 [2, 8, 64], P(None, 'tx', 'ty'), may hold values 0 or 1
- coeffs: float32 [5], replicated, may hold values from -1 to 1
Outputs:
- torque: float32 [8, 64, 64], P('tx', 'ty')
The draws below stay inside these ranges and needn't reach their ends.
All inputs are finite; a program needn't handle non-finite values. No bound on the sum of `bond_mask` on one device may be relied on, other than what follows from the above.
Results may differ from the reference program's by a relative error of at most 0.03.
Values may be sent and summed in bfloat16 or wider, within the bound.
No kernel may reach another device: no remote copies, remote signals or barrier semaphores. Data moves between devices by JAX's collectives and lax.ppermute only.
A program may use at most 64 MiB of HBM per device.

```python
import jax
import jax.numpy as jnp
from jax import lax

ORB = 128
SITES = 64
PROBES = 64
STEPS = 4
NCR = 8
NCC = 64


def place_ends(entries, key, least, high):
    longest = entries.shape.index(max(entries.shape))
    spots = []
    for shift in (0, 1):
        where = [jax.random.randint(jax.random.fold_in(key, axis), (), 0, length) for axis, length in enumerate(entries.shape)]
        where[longest] = (where[longest] + shift) % entries.shape[longest]
        spots.append(tuple(where))
    return entries.at[spots[0]].set(least).at[spots[1]].set(high)


def levels(rng, shape, pieces, smallest, largest):
    gain, own = 1.0, jax.random.fold_in(rng, 6)
    for axis_at, blocks in pieces:
        steps = jnp.exp(jax.random.uniform(jax.random.fold_in(own, axis_at), (blocks,), jnp.float32, smallest / len(pieces), largest / len(pieces)))
        gain = gain * jnp.repeat(steps, shape[axis_at] // blocks).reshape([-1 if axis == axis_at else 1 for axis in range(len(shape))])
    return gain


def normal_values(key, extent, scale, bound, pieces=(), dtype=jnp.bfloat16):
    drawn = scale * jax.random.normal(key, extent, jnp.float32)
    if pieces:
        drawn = drawn * levels(key, extent, pieces, -0.22, 0.18)
    return jnp.clip(drawn, -bound, bound).astype(dtype)


def setup_inputs(seed: int = 0) -> dict:
    keys = jax.random.split(jax.random.key(seed), 9)
    return {
        "probes": normal_values(keys[0], (NCR, NCC, PROBES, ORB), 1.0, 6.0, ((0, 8), (1, 4))),
        "left_probes": normal_values(keys[1], (NCR, NCC, PROBES, ORB), 1.0, 6.0, ((0, 8), (1, 4))),
        "angles": jnp.clip(jax.random.uniform(keys[2], (NCR, NCC, SITES), jnp.float32, -3.140625, 3.140625), -3.140625, 3.140625),
        "cluster_hopping": normal_values(keys[3], (NCR, NCC, ORB, ORB), (64 * ORB) ** -0.5, 0.0625, ((0, 8), (1, 4))),
        "east_bonds": normal_values(keys[4], (NCR, NCC, ORB, ORB), (128 * ORB) ** -0.5, 0.046875, ((0, 8), (1, 4))),
        "south_bonds": normal_values(keys[5], (NCR, NCC, ORB, ORB), (128 * ORB) ** -0.5, 0.046875, ((0, 8), (1, 4))),
        "bond_mask": place_ends((jax.random.randint(keys[6], (2, NCR, NCC), 0, 4) < 3).astype(jnp.int32), jax.random.fold_in(keys[6], 1), 0, 1),
        "coeffs": jnp.clip(jax.random.uniform(keys[7], (STEPS + 1,), jnp.float32, -1.0, 1.0), -1.0, 1.0),
    }


coupling = 0.5


def onsite_matrix(angles):
    orbs = 2 * angles.shape[-1]
    index = jnp.arange(orbs)
    spin_sign = jnp.where(index % 2 == 0, 1.0, -1.0).astype(jnp.float32)
    same_site = (index[:, None] // 2) == (index[None, :] // 2)
    same_orbital = index[:, None] == index[None, :]
    cosine = jnp.repeat(jnp.cos(angles), 2, axis=-1)[..., :, None]
    sine_rep = jnp.repeat(jnp.sin(angles), 2, axis=-1)[..., :, None]
    diag_part = jnp.where(same_orbital, spin_sign[:, None] * cosine, 0.0)
    cross_part = jnp.where(same_site & (~same_orbital), sine_rep, 0.0)
    return coupling * (diag_part + cross_part)


def to_float(array):
    return array.astype(jnp.float32)


def apply_rows(vectors, diag_block, east_block, south_block):
    total_rows = vectors.shape[0]

    def one_row(row_index):
        above = (row_index - 1) % total_rows
        below = (row_index + 1) % total_rows
        centre = to_float(vectors[row_index])
        east_side = jnp.roll(centre, -1, axis=0)
        west_side = jnp.roll(centre, 1, axis=0)
        south_side = to_float(vectors[below])
        north_side = to_float(vectors[above])
        bond_row = to_float(east_block[row_index])
        west_bond = jnp.roll(bond_row, 1, axis=0)
        result = jnp.einsum("qrk,qjk->qrj", centre, to_float(diag_block[row_index]))
        result = result + jnp.einsum("qrk,qik->qri", east_side, bond_row)
        result = result + jnp.einsum("qrk,qki->qri", west_side, west_bond)
        result = result + jnp.einsum("qrk,qik->qri", south_side, to_float(south_block[row_index]))
        result = result + jnp.einsum("qrk,qki->qri", north_side, to_float(south_block[above]))
        return result

    return lax.map(one_row, jnp.arange(total_rows))


def reference(probes, left_probes, angles, cluster_hopping, east_bonds, south_bonds, bond_mask, coeffs):
    def build_row(row_index):
        hopping = to_float(cluster_hopping[row_index])
        total = hopping + jnp.swapaxes(hopping, 1, 2) + onsite_matrix(angles[row_index])
        return total.astype(jnp.bfloat16)

    diag_block = lax.map(build_row, jnp.arange(probes.shape[0]))
    east_block = east_bonds * bond_mask[0][:, :, None, None].astype(jnp.bfloat16)
    south_block = south_bonds * bond_mask[1][:, :, None, None].astype(jnp.bfloat16)

    def apply_h(vectors):
        return apply_rows(vectors, diag_block, east_block, south_block)

    forward = [probes, apply_h(probes).astype(jnp.bfloat16)]
    for level in range(1, STEPS):
        nxt = 2.0 * apply_h(forward[level]) - to_float(forward[level - 1])
        forward.append(nxt.astype(jnp.bfloat16))
    base = to_float(left_probes)
    adjoint = {}
    adjoint[STEPS + 1] = (coeffs[STEPS] * base).astype(jnp.bfloat16)
    adjoint[STEPS] = (coeffs[STEPS - 1] * base + 2.0 * apply_h(adjoint[STEPS + 1])).astype(jnp.bfloat16)
    for level in range(STEPS - 1, 0, -1):
        value = coeffs[level - 1] * base + 2.0 * apply_h(adjoint[level + 1]) - to_float(adjoint[level + 2])
        adjoint[level] = value.astype(jnp.bfloat16)

    shape = probes.shape
    def split_spin(array):
        return to_float(array).reshape(shape[0], shape[1], shape[2], shape[3] // 2, 2)

    pair = jnp.einsum("pqrsa,pqrsb->pqsab", split_spin(adjoint[1]), split_spin(forward[0]))
    for level in range(1, STEPS + 1):
        pair = pair + 2.0 * jnp.einsum("pqrsa,pqrsb->pqsab", split_spin(adjoint[level + 1]), split_spin(forward[level]))
    pair = pair / shape[2]
    torque = coupling * (jnp.sin(angles) * (pair[..., 0, 0] - pair[..., 1, 1]) - jnp.cos(angles) * (pair[..., 0, 1] + pair[..., 1, 0]))
    return torque
```

```python
import jax
import jax.numpy as jnp
from jax import lax
from jax.experimental import pallas as pl
from jax.experimental.pallas import tpu as pltpu
from jax.sharding import PartitionSpec as P

coupling = 0.5
F32 = jnp.float32
BF16 = jnp.bfloat16
VM = pl.BlockSpec(memory_space=pltpu.VMEM)
SM = pl.BlockSpec(memory_space=pltpu.SMEM)
HIGH = lax.Precision.HIGHEST


def mm(x, y):
    return lax.dot_general(x, y, (((1,), (0,)), ((), ())), preferred_element_type=F32)


def mm_t(x, y):
    return lax.dot_general(x, y, (((1,), (1,)), ((), ())), preferred_element_type=F32)


def call(body, outs, *args, specs=None, flops=0):
    specs = specs or [VM] * len(args)
    nbytes = sum(a.size * a.dtype.itemsize for a in args) + sum(
        o.size * o.dtype.itemsize for o in outs
    )
    return pl.pallas_call(
        body,
        out_shape=tuple(outs),
        in_specs=specs,
        out_specs=tuple(VM for _ in outs),
        cost_estimate=pl.CostEstimate(flops=flops, transcendentals=0, bytes_accessed=nbytes),
        compiler_params=pltpu.CompilerParams(vmem_limit_bytes=32 * 1024 * 1024),
    )(*args)


def sds(shape, dtype):
    return jax.ShapeDtypeStruct(shape, dtype)


def lane_grid(rows, cols):
    return (
        lax.broadcasted_iota(jnp.int32, (rows, cols), 0),
        lax.broadcasted_iota(jnp.int32, (rows, cols), 1),
    )


def swap_matrix(orbs):
    row, col = lane_grid(orbs, orbs)
    partner = col + 1 - 2 * (col % 2)
    return jnp.where(row == partner, 1.0, 0.0).astype(BF16)


def diag_kernel(hop_ref, east_ref, cos_ref, sin_ref, diag_ref, east_t_ref):
    cols, orbs = hop_ref.shape[0], hop_ref.shape[1]
    site, lane = lane_grid(orbs // 2, orbs)
    spread = jnp.where(site == lane // 2, 1.0, 0.0)
    signed = jnp.where(lane % 2 == 0, spread, -spread)
    cosine = coupling * jnp.dot(cos_ref[...], signed, precision=HIGH, preferred_element_type=F32)
    sine = coupling * jnp.dot(sin_ref[...], spread, precision=HIGH, preferred_element_type=F32)
    row, col = lane_grid(orbs, orbs)
    on_diag = row == col
    crossed = row == col + 1 - 2 * (col % 2)
    for c in range(cols):
        hop = hop_ref[c].astype(F32)
        onsite = jnp.where(on_diag, cosine[c : c + 1], 0.0)
        onsite = jnp.where(crossed, sine[c : c + 1], onsite)
        diag_ref[c] = (hop + hop.T + onsite).astype(BF16)
        east_t_ref[c] = east_ref[c].astype(F32).T.astype(BF16)


def vertical_kernel(side_ref, own_ref, north_ref, plo_ref, phi_ref, olo_ref, ohi_ref):
    half = plo_ref.shape[0]
    partner_refs, other_refs = ((plo_ref, phi_ref), (olo_ref, ohi_ref))

    def fill(south_refs, north_refs):
        for c in range(2 * half):
            south_refs[c // half][c % half] = own_ref[c].astype(F32).T.astype(BF16)
            north_refs[c // half][c % half] = north_ref[c]

    @pl.when(side_ref[0] == 0)
    def _():
        fill(partner_refs, other_refs)

    @pl.when(side_ref[0] != 0)
    def _():
        fill(other_refs, partner_refs)


def along_row(c, cols, lo_ref, hi_ref, west_ref, east_ref, diag_ref, east_t_ref, em_ref, ew_ref):
    half = cols // 2

    def block(index):
        return lo_ref[index] if index < half else hi_ref[index - half]

    total = mm(block(c), diag_ref[c])
    total = total + mm(block(c + 1) if c + 1 < cols else east_ref[0], east_t_ref[c])
    total = total + mm(
        block(c - 1) if c > 0 else west_ref[0], em_ref[c - 1] if c > 0 else ew_ref[0]
    )
    return total


def row_kernel(coeff_ref, *refs, factor, level, has_prev):
    refs = list(refs)
    row_refs = [refs.pop(0) for _ in range(8)]
    prev_refs = [refs.pop(0) for _ in range(2)] if has_prev else None
    base_ref = refs.pop(0) if level is not None else None
    outs = refs
    cols = row_refs[4].shape[0]
    half = cols // 2
    for c in range(cols):
        total = along_row(c, cols, *row_refs)
        total = factor * total
        if base_ref is not None:
            total = total + coeff_ref[level] * base_ref[c].astype(F32)
        if has_prev:
            total = total - prev_refs[c // half][c % half].astype(F32)
        outs[c // half][c % half] = total


def column_kernel(part_ref, partner_ref, other_ref, pm_ref, om_ref, out_ref, *, factor):
    for c in range(part_ref.shape[0]):
        total = mm(partner_ref[c], pm_ref[c]) + mm(other_ref[c], om_ref[c])
        out_ref[c] = (part_ref[c] + factor * total).astype(BF16)


def far_kernel(
    alo, ahi, glo, ghi, mlo, mhi, plo, phi, llo, lhi, out_ref
):
    half, orbs = alo.shape[0], alo.shape[2]
    swap = swap_matrix(orbs)
    for c in range(2 * half):
        i = c % half
        a, g, m, p, left = [
            (x if c < half else y)[i]
            for x, y in ((alo, ahi), (glo, ghi), (mlo, mhi), (plo, phi), (llo, lhi))
        ]
        moved_a = 4.0 * mm_t(a, m)
        moved_g = 2.0 * mm_t(g, m)
        same = moved_g * p.astype(F32) + moved_a * left.astype(F32)
        cross = moved_g * mm(p, swap) + moved_a * mm(left, swap)
        out_ref[c : c + 1, :] = jnp.sum(same, axis=0, keepdims=True)
        out_ref[2 * half + c : 2 * half + c + 1, :] = jnp.sum(cross, axis=0, keepdims=True)


def near_kernel(coeff_ref, *refs):
    refs = list(refs)
    ops = [refs.pop(0) for _ in range(4)]
    a3_halo = [refs.pop(0) for _ in range(2)]
    g2_halo = [refs.pop(0) for _ in range(2)]
    forward = [[refs.pop(0) for _ in range(2)] for _ in range(4)]
    adjoint = [[refs.pop(0) for _ in range(2)] for _ in range(4)]
    base_ref, out_ref = refs
    cols, orbs = ops[0].shape[0], ops[0].shape[1]
    half = cols // 2
    swap = swap_matrix(orbs)
    for c in range(cols):
        a = [pair[c // half][c % half] for pair in forward]
        g = [pair[c // half][c % half] for pair in adjoint]
        last_a = 2.0 * along_row(c, cols, *forward[3], *a3_halo, *ops) - a[2].astype(F32)
        last_g = 2.0 * along_row(c, cols, *adjoint[0], *g2_halo, *ops) - g[1].astype(F32)
        last_g = last_g + coeff_ref[0] * base_ref[c].astype(F32)
        same = last_g * a[0].astype(F32)
        cross = last_g * mm(a[0], swap)
        same2 = last_a * g[3].astype(F32)
        cross2 = last_a * mm(g[3], swap)
        for n in range(3):
            same2 = same2 + g[n].astype(F32) * a[n + 1].astype(F32)
            cross2 = cross2 + g[n].astype(F32) * mm(a[n + 1], swap)
        out_ref[c : c + 1, :] = jnp.sum(same + 2.0 * same2, axis=0, keepdims=True)
        out_ref[cols + c : cols + c + 1, :] = jnp.sum(cross + 2.0 * cross2, axis=0, keepdims=True)


def torque_kernel(near_ref, partner_ref, other_ref, cos_ref, sin_ref, out_ref, *, scale):
    total = near_ref[...] + partner_ref[...] + other_ref[...]
    cols, orbs = total.shape[0] // 2, total.shape[1]
    lane, site = lane_grid(orbs, orbs // 2)
    gather = jnp.where(lane // 2 == site, 1.0, 0.0)
    signed = jnp.where(lane % 2 == 0, gather, -gather)
    spin_diff = jnp.dot(total[:cols], signed, precision=HIGH, preferred_element_type=F32)
    spin_mix = jnp.dot(total[cols:], gather, precision=HIGH, preferred_element_type=F32)
    out_ref[...] = (coupling * scale) * (sin_ref[...] * spin_diff - cos_ref[...] * spin_mix)


def on_device(
    probes, left_probes, angles, cluster_hopping, east_bonds, south_bonds, bond_mask, coeffs
):
    rows, columns = (lax.axis_size("tx"), lax.axis_size("ty"))
    flip = [(i, i ^ 1) for i in range(rows)]
    onward = [(i, (i + 2) % rows if i % 2 == 0 else (i - 2) % rows) for i in range(rows)]
    outer = [(i, (i - 1) % rows if i % 2 == 0 else (i + 1) % rows) for i in range(rows)]
    south = [(i, (i + 1) % rows) for i in range(rows)]
    east = [(i, (i + 1) % columns) for i in range(columns)]
    west = [(j, i) for i, j in east]
    side = (lax.axis_index("tx") % 2).astype(jnp.int32).reshape(1)

    probes, left, angles = probes[0], left_probes[0], angles[0]
    hop, ebond, sbond = cluster_hopping[0], east_bonds[0], south_bonds[0]
    cols, count, orbs = probes.shape
    half = cols // 2
    vec = sds((half, count, orbs), BF16)
    vec32 = sds((half, count, orbs), F32)
    mat = sds((half, orbs, orbs), BF16)

    def exchange(lo, hi):
        partner = [lax.ppermute(x, "tx", flip) for x in (lo, hi)]
        other = [lax.ppermute(x, "tx", onward) for x in partner]
        return partner, other

    def halo(lo, hi):
        return (
            lax.ppermute(hi[half - 1 :], "ty", east),
            lax.ppermute(lo[:1], "ty", west),
        )

    a0 = [probes[:half], probes[half:]]
    g5_all = (coeffs[4] * left.astype(F32)).astype(BF16)
    g5 = [g5_all[:half], g5_all[half:]]
    south_own = sbond * bond_mask[1, 0][:, None, None].astype(BF16)
    east_own = ebond * bond_mask[0, 0][:, None, None].astype(BF16)
    a0_near, a0_far = exchange(*a0)
    south_in = lax.ppermute(south_own, "tx", south)
    g5_near, g5_far = exchange(*g5)
    east_in = lax.ppermute(east_own[cols - 1 :], "ty", east)
    cosine, sine = jnp.cos(angles), jnp.sin(angles)
    big = sds((cols, orbs, orbs), BF16)
    diag, east_t = call(diag_kernel, (big, big), hop, east_own, cosine, sine)
    plo, phi, olo, ohi = call(
        vertical_kernel, (mat,) * 4, side, south_own, south_in, specs=[SM, VM, VM]
    )
    operators = (diag, east_t, east_own, east_in)
    unit = 2 * count * orbs * orbs

    def along(pair, edges, factor, prev=None, level=None):
        def body(*refs):
            row_kernel(*refs, factor=factor, level=level, has_prev=prev is not None)

        extra = list(prev) if prev is not None else []
        if level is not None:
            extra = extra + [left]
        args = [coeffs, *pair, *edges, *operators, *extra]
        return call(
            body,
            (vec32, vec32),
            *args,
            specs=[SM] + [VM] * (len(args) - 1),
            flops=3 * cols * unit,
        )

    def across(parts, near, far, factor):
        def body(*refs):
            column_kernel(*refs, factor=factor)

        return [
            call(body, (vec,), part, n, f, p, o, flops=2 * half * unit)[0]
            for part, n, f, p, o in zip(parts, near, far, (plo, phi), (olo, ohi))
        ]

    a1 = across(along(a0, halo(*a0), 1.0), a0_near, a0_far, 1.0)
    g4 = across(along(g5, halo(*g5), 2.0, level=3), g5_near, g5_far, 2.0)

    def step(pair, prev, level=None):
        near, far = exchange(*pair)
        return across(along(pair, halo(*pair), 2.0, prev, level), near, far, 2.0)

    a2 = step(a1, a0)
    g3 = step(g4, g5, 2)
    a3 = step(a2, a1)
    g2 = step(g3, g4, 1)
    edges = (*halo(*a3), *halo(*g2))
    sums = sds((2 * cols, orbs), F32)
    (to_partner,) = call(
        far_kernel, (sums,), *a3, *g2, plo, phi, *a0_near, *g5_near, flops=4 * cols * unit
    )
    (to_other,) = call(
        far_kernel, (sums,), *a3, *g2, olo, ohi, *a0_far, *g5_far, flops=4 * cols * unit
    )
    from_partner = lax.ppermute(to_partner, "tx", flip)
    from_other = lax.ppermute(to_other, "tx", outer)
    args = [coeffs, *operators, *edges, *a0, *a1, *a2, *a3, *g2, *g3, *g4, *g5, left]
    (own,) = call(
        near_kernel, (sums,), *args, specs=[SM] + [VM] * (len(args) - 1), flops=11 * cols * unit
    )

    def finish(*refs):
        torque_kernel(*refs, scale=1.0 / count)

    (torque,) = call(
        finish, (sds((cols, orbs // 2), F32),), own, from_partner, from_other, cosine, sine
    )
    return torque[None]


def solution(mesh):
    placed = (
        P("tx", "ty", None, None),
        P("tx", "ty", None, None),
        P("tx", "ty", None),
        P("tx", "ty", None, None),
        P("tx", "ty", None, None),
        P("tx", "ty", None, None),
        P(None, "tx", "ty"),
        P(),
    )
    return jax.shard_map(
        on_device, mesh=mesh, in_specs=placed, out_specs=P("tx", "ty", None), check_vma=False
    )
```

```python
import jax
import jax.numpy as jnp
from jax import lax
from jax.experimental import pallas as pl
from jax.experimental.pallas import tpu as pltpu
from jax.sharding import PartitionSpec as P

coupling = 0.5
CHUNKS = 4
F32 = jnp.float32
BF16 = jnp.bfloat16
VM = pl.BlockSpec(memory_space=pltpu.VMEM)
SM = pl.BlockSpec(memory_space=pltpu.SMEM)
HIGH = lax.Precision.HIGHEST


def mm(x, y):
    return lax.dot_general(x, y, (((1,), (0,)), ((), ())), preferred_element_type=F32)


def mm_t(x, y):
    return lax.dot_general(x, y, (((1,), (1,)), ((), ())), preferred_element_type=F32)


def sds(shape, dtype):
    return jax.ShapeDtypeStruct(tuple(shape), dtype)


def call(body, outs, *args, scalars=1, flops=0):
    nbytes = sum(a.size * a.dtype.itemsize for a in (*args, *outs))
    return pl.pallas_call(
        body,
        out_shape=tuple(outs),
        in_specs=[SM] * scalars + [VM] * (len(args) - scalars),
        out_specs=tuple(VM for _ in outs),
        cost_estimate=pl.CostEstimate(flops=flops, transcendentals=0, bytes_accessed=nbytes),
        compiler_params=pltpu.CompilerParams(vmem_limit_bytes=32 * 1024 * 1024),
    )(*args)


def lane_grid(rows, cols):
    return (
        lax.broadcasted_iota(jnp.int32, (rows, cols), 0),
        lax.broadcasted_iota(jnp.int32, (rows, cols), 1),
    )


def swap_matrix(orbs):
    row, col = lane_grid(orbs, orbs)
    return jnp.where(row == col + 1 - 2 * (col % 2), 1.0, 0.0).astype(BF16)


def scaled(coeff, value):
    return (coeff * value.astype(F32)).astype(BF16)


def take(refs):
    def some(count):
        return [refs.pop(0) for _ in range(count)]

    return some


def diag_kernel(
    mask_ref, hop_ref, east_ref, edge_ref, cos_ref, sin_ref,
    diag_ref, east_t_ref, east_m_ref, signed_sin_ref, cos_out_ref, *, scale
):
    cols, orbs = hop_ref.shape[0], hop_ref.shape[1]
    site, lane = lane_grid(orbs // 2, orbs)
    spread = jnp.where(site == lane // 2, coupling, 0.0)
    signed = jnp.where(lane % 2 == 0, spread, -spread)
    cosine = jnp.dot(cos_ref[...], spread, precision=HIGH, preferred_element_type=F32)
    sine = jnp.dot(sin_ref[...], spread, precision=HIGH, preferred_element_type=F32)
    sign = jnp.where(lane[:1] % 2 == 0, 1.0, -1.0)
    signed_sin_ref[...] = scale * sign * sine
    cos_out_ref[...] = scale * cosine
    cosine = sign * cosine
    row, col = lane_grid(orbs, orbs)
    on_diag = row == col
    crossed = row == col + 1 - 2 * (col % 2)
    east_m_ref[0] = edge_ref[0]
    for c in range(cols):
        hop = hop_ref[c].astype(F32)
        onsite = jnp.where(on_diag, cosine[c : c + 1], 0.0)
        onsite = jnp.where(crossed, sine[c : c + 1], onsite)
        diag_ref[c] = (hop + hop.T + onsite).astype(BF16)
        east = east_ref[c].astype(F32) * mask_ref[c].astype(F32)
        east_t_ref[c] = east.T.astype(BF16)
        if c + 1 < cols:
            east_m_ref[c + 1] = east.astype(BF16)


def vertical_kernel(side_ref, own_ref, north_ref, partner_ref, other_ref):
    def fill(south_out, north_out):
        for c in range(own_ref.shape[0]):
            south_out[c] = own_ref[c].astype(F32).T.astype(BF16)
            north_out[c] = north_ref[c]

    @pl.when(side_ref[0] == 0)
    def _():
        fill(partner_ref, other_ref)

    @pl.when(side_ref[0] != 0)
    def _():
        fill(other_ref, partner_ref)


def both(ref, c):
    block = ref[:, c]
    return block.reshape(block.shape[0] * block.shape[1], block.shape[2])


def along_row(c, block, edge_refs, ops):
    diag_ref, east_t_ref, east_m_ref = ops
    cols = diag_ref.shape[0]

    def flat(ref):
        value = ref[...]
        return value.reshape(value.shape[0] * value.shape[1], value.shape[2])

    east = block(c + 1) if c + 1 < cols else flat(edge_refs[1])
    west = block(c - 1) if c > 0 else flat(edge_refs[0])
    total = mm(block(c), diag_ref[c])
    return total + mm(east, east_t_ref[c]) + mm(west, east_m_ref[c])


def first_row_kernel(coeff_ref, *refs, width):
    some = take(list(refs))
    ops, edges, (probe_ref, left_ref) = some(3), some(2), some(2)
    outs = some(len(refs) - 7)
    cols, count = probe_ref.shape[0], probe_ref.shape[1]
    top = coeff_ref[coeff_ref.shape[0] - 1]

    def block(c):
        return jnp.concatenate([probe_ref[c], scaled(top, left_ref[c])], axis=0)

    edge_values = []
    for ref in edges:
        edge_values.append(jnp.concatenate([ref[0], scaled(top, ref[1])], axis=0)[None])
    blocks = [block(c) for c in range(cols)]
    for c in range(cols):
        total = along_row(c, lambda i: blocks[i], edge_values, ops)
        base = coeff_ref[3] * left_ref[c].astype(F32)
        outs[c // width][0, c % width] = total[:count]
        outs[c // width][1, c % width] = 2.0 * total[count:] + base


def row_kernel(coeff_ref, *refs, width, level, first):
    some = take(list(refs))
    ops, edges, (left_ref,) = some(3), some(2), some(1)
    cols = left_ref.shape[0]
    chunks = cols // width
    states = some(chunks)
    prevs = some(1) if first else some(chunks)
    outs = some(chunks)
    count = left_ref.shape[1]

    def block(c):
        return both(states[c // width], c % width)

    for c in range(cols):
        k, i = divmod(c, width)
        total = 2.0 * along_row(c, block, edges, ops)
        if first:
            old_a = prevs[0][c]
            old_g = scaled(coeff_ref[coeff_ref.shape[0] - 1], left_ref[c])
        else:
            old_a, old_g = prevs[k][0, i], prevs[k][1, i]
        base = coeff_ref[level] * left_ref[c].astype(F32)
        outs[k][0, i] = total[:count] - old_a.astype(F32)
        outs[k][1, i] = total[count:] + base - old_g.astype(F32)


def column_kernel(coeff_ref, *refs, start, first):
    some = take(list(refs))
    ops, (part_ref,) = some(2), some(1)
    moved = some(4 if first else 2)
    out_ref, *edge = some(len(refs) - 3 - len(moved))
    width, count = part_ref.shape[1], part_ref.shape[2]
    top = coeff_ref[coeff_ref.shape[0] - 1]
    for i in range(width):
        c = start + i
        if first:
            near, far = [
                jnp.concatenate([a[c], scaled(top, g[c])], axis=0)
                for a, g in (moved[:2], moved[2:])
            ]
        else:
            near, far = both(moved[0], i), both(moved[1], i)
        total = mm(near, ops[0][c]) + mm(far, ops[1][c])
        factor = 1.0 if first else 2.0
        new_a = (part_ref[0, i] + factor * total[:count]).astype(BF16)
        new_g = (part_ref[1, i] + 2.0 * total[count:]).astype(BF16)
        out_ref[0, i] = new_a
        out_ref[1, i] = new_g
        if edge and i == (0 if start == 0 else width - 1):
            edge[0][0] = new_a
            edge[0][1] = new_g


def far_kernel(coeff_ref, *refs, width):
    some = take(list(refs))
    (op_ref, probe_ref, left_ref) = some(3)
    cols, count, orbs = probe_ref.shape
    states = some(cols // width)
    (out_ref,) = some(1)
    top = coeff_ref[coeff_ref.shape[0] - 1]
    swap = swap_matrix(orbs)
    for c in range(cols):
        moved = mm_t(both(states[c // width], c % width), op_ref[c])
        moved_a, moved_g = 4.0 * moved[:count], 2.0 * moved[count:]
        p, left = probe_ref[c], scaled(top, left_ref[c])
        same = moved_g * p.astype(F32) + moved_a * left.astype(F32)
        cross = moved_g * mm(p, swap) + moved_a * mm(left, swap)
        out_ref[c : c + 1, :] = jnp.sum(same, axis=0, keepdims=True)
        out_ref[cols + c : cols + c + 1, :] = jnp.sum(cross, axis=0, keepdims=True)


def near_kernel(coeff_ref, *refs, width):
    some = take(list(refs))
    ops, edges, (probe_ref, left_ref) = some(3), some(2), some(2)
    cols, count, orbs = probe_ref.shape
    chunks = cols // width
    first, second, third = some(chunks), some(chunks), some(chunks)
    (out_ref,) = some(1)
    top = coeff_ref[coeff_ref.shape[0] - 1]
    swap = swap_matrix(orbs)

    def block(c):
        return both(third[c // width], c % width)

    for c in range(cols):
        k, i = divmod(c, width)
        a = [probe_ref[c], first[k][0, i], second[k][0, i], third[k][0, i]]
        g = [third[k][1, i], second[k][1, i], first[k][1, i], scaled(top, left_ref[c])]
        total = 2.0 * along_row(c, block, edges, ops)
        last_a = total[:count] - a[2].astype(F32)
        last_g = total[count:] + coeff_ref[0] * left_ref[c].astype(F32) - g[1].astype(F32)
        same = last_g * a[0].astype(F32)
        cross = last_g * mm(a[0], swap)
        same2 = last_a * g[3].astype(F32)
        cross2 = last_a * mm(g[3], swap)
        for n in range(3):
            same2 = same2 + g[n].astype(F32) * a[n + 1].astype(F32)
            cross2 = cross2 + g[n].astype(F32) * mm(a[n + 1], swap)
        out_ref[c : c + 1, :] = jnp.sum(same + 2.0 * same2, axis=0, keepdims=True)
        out_ref[cols + c : cols + c + 1, :] = jnp.sum(cross + 2.0 * cross2, axis=0, keepdims=True)


def torque_kernel(near_ref, partner_ref, other_ref, sin_ref, cos_ref, out_ref):
    total = near_ref[...] + partner_ref[...] + other_ref[...]
    cols, orbs = total.shape[0] // 2, total.shape[1]
    lane, site = lane_grid(orbs, orbs // 2)
    gather = jnp.where(lane // 2 == site, 1.0, 0.0)
    lanes = sin_ref[...] * total[:cols] - cos_ref[...] * total[cols:]
    out_ref[...] = jnp.dot(lanes, gather, precision=HIGH, preferred_element_type=F32)


def on_device(
    probes, left_probes, angles, cluster_hopping, east_bonds, south_bonds, bond_mask, coeffs
):
    rows, columns = (lax.axis_size("tx"), lax.axis_size("ty"))
    flip = [(i, i ^ 1) for i in range(rows)]
    onward = [(i, (i + 2) % rows if i % 2 == 0 else (i - 2) % rows) for i in range(rows)]
    outer = [(i, (i - 1) % rows if i % 2 == 0 else (i + 1) % rows) for i in range(rows)]
    south = [(i, (i + 1) % rows) for i in range(rows)]
    east = [(i, (i + 1) % columns) for i in range(columns)]
    west = [(j, i) for i, j in east]
    side = (lax.axis_index("tx") % 2).astype(jnp.int32).reshape(1)

    probes, left, angles = probes[0], left_probes[0], angles[0]
    hop, ebond, sbond = cluster_hopping[0], east_bonds[0], south_bonds[0]
    cols, count, orbs = probes.shape
    width = cols // CHUNKS
    order = [0, CHUNKS - 1, *range(1, CHUNKS - 1)]
    unit = 4 * count * orbs * orbs

    near_p = lax.ppermute(probes, "tx", flip)
    near_l = lax.ppermute(left, "tx", flip)
    east_edge = jnp.stack([probes[cols - 1], left[cols - 1]])
    west_edge = jnp.stack([probes[0], left[0]])
    edges = (lax.ppermute(east_edge, "ty", east), lax.ppermute(west_edge, "ty", west))
    far_p = lax.ppermute(near_p, "tx", onward)
    south_own = jnp.where(bond_mask[1, 0][:, None, None] != 0, sbond, jnp.zeros_like(sbond))
    south_send, _ = lax.optimization_barrier((south_own, near_p))
    south_in = lax.ppermute(south_send, "tx", south)
    far_l = lax.ppermute(near_l, "tx", onward)
    last_bond = jnp.where(bond_mask[0, 0, cols - 1] != 0, ebond[cols - 1 :], 0).astype(BF16)
    east_in = lax.ppermute(last_bond, "ty", east)

    big = sds((cols, orbs, orbs), BF16)
    lanes = sds((cols, orbs), F32)

    def build(*refs):
        diag_kernel(*refs, scale=1.0 / count)

    diag, east_t, east_m, sine, cosine = call(
        build, (big, big, big, lanes, lanes),
        bond_mask[0, 0], hop, ebond, east_in, jnp.cos(angles), jnp.sin(angles),
    )
    near_m, far_m = call(vertical_kernel, (big, big), side, south_own, south_in)
    ops = (diag, east_t, east_m)
    part = sds((2, width, count, orbs), F32)
    state = sds((2, width, count, orbs), BF16)
    edge = sds((2, count, orbs), BF16)

    def across(parts, moved, first):
        out, ends = [None] * CHUNKS, {}
        for k in order:
            start = k * width

            def body(*refs, start=start):
                column_kernel(*refs, start=start, first=first)

            shapes = (state, edge) if k in (0, CHUNKS - 1) else (state,)
            out[k], *more = call(
                body, shapes, coeffs, near_m, far_m, parts[k], *moved[k], flops=2 * width * unit
            )
            if more:
                ends[k] = more[0]
        return out, ends[0], ends[CHUNKS - 1]

    def first_row(*refs):
        first_row_kernel(*refs, width=width)

    parts = call(
        first_row, (part,) * CHUNKS, coeffs, *ops, *edges, probes, left, flops=3 * cols * unit
    )
    now, low, high = across(parts, [(near_p, near_l, far_p, far_l)] * CHUNKS, True)
    states = [now]
    for n in (1, 2):
        near, far = [None] * CHUNKS, [None] * CHUNKS
        for k in order:
            near[k] = lax.ppermute(now[k], "tx", flip)
        edges = (lax.ppermute(high, "ty", east), lax.ppermute(low, "ty", west))
        for k in order:
            send = near[k]
            if k == order[-1]:
                send, *edges = lax.optimization_barrier((send, *edges))
            far[k] = lax.ppermute(send, "tx", onward)

        def body(*refs, n=n):
            row_kernel(*refs, width=width, level=3 - n, first=n == 1)

        prev = [probes] if n == 1 else states[-2]
        parts = call(
            body, (part,) * CHUNKS, coeffs, *ops, *edges, left, *now, *prev,
            flops=3 * cols * unit,
        )
        now, low, high = across(parts, list(zip(near, far)), False)
        states.append(now)

    edges = (lax.ppermute(high, "ty", east), lax.ppermute(low, "ty", west))
    sums = sds((2 * cols, orbs), F32)

    def far_sums(*refs):
        far_kernel(*refs, width=width)

    def near_sums(*refs):
        near_kernel(*refs, width=width)

    (to_other,) = call(far_sums, (sums,), coeffs, far_m, far_p, far_l, *now, flops=2 * cols * unit)
    (to_partner,) = call(
        far_sums, (sums,), coeffs, near_m, near_p, near_l, *now, flops=2 * cols * unit
    )
    from_other = lax.ppermute(to_other, "tx", outer)
    from_partner = lax.ppermute(to_partner, "tx", flip)
    (own,) = call(
        near_sums, (sums,), coeffs, *ops, *edges, probes, left, *states[0], *states[1], *now,
        flops=6 * cols * unit,
    )
    (torque,) = call(
        torque_kernel, (sds((cols, orbs // 2), F32),),
        own, from_partner, from_other, sine, cosine, scalars=0,
    )
    return torque[None]


def solution(mesh):
    placed = (
        P("tx", "ty", None, None),
        P("tx", "ty", None, None),
        P("tx", "ty", None),
        P("tx", "ty", None, None),
        P("tx", "ty", None, None),
        P("tx", "ty", None, None),
        P(None, "tx", "ty"),
        P(),
    )
    return jax.shard_map(
        on_device, mesh=mesh, in_specs=placed, out_specs=P("tx", "ty", None), check_vma=False
    )
```

```python
import jax
import jax.numpy as jnp
from jax import lax
from jax.experimental import pallas as pl
from jax.experimental.pallas import tpu as pltpu
from jax.sharding import PartitionSpec as P

coupling = 0.5
CHUNKS = 4
F32 = jnp.float32
BF16 = jnp.bfloat16
VM = pl.BlockSpec(memory_space=pltpu.VMEM)
SM = pl.BlockSpec(memory_space=pltpu.SMEM)
HIGH = lax.Precision.HIGHEST


def mm(x, y):
    return lax.dot_general(x, y, (((1,), (0,)), ((), ())), preferred_element_type=F32)


def mm_t(x, y):
    return lax.dot_general(x, y, (((1,), (1,)), ((), ())), preferred_element_type=F32)


def sds(shape, dtype):
    return jax.ShapeDtypeStruct(tuple(shape), dtype)


def call(body, outs, *args, scalars=0, flops=0):
    nbytes = sum(a.size * a.dtype.itemsize for a in (*args, *outs))
    return pl.pallas_call(
        body,
        out_shape=tuple(outs),
        in_specs=[SM] * scalars + [VM] * (len(args) - scalars),
        out_specs=tuple(VM for _ in outs),
        cost_estimate=pl.CostEstimate(flops=flops, transcendentals=0, bytes_accessed=nbytes),
        compiler_params=pltpu.CompilerParams(vmem_limit_bytes=32 * 1024 * 1024),
    )(*args)


def lane_grid(rows, cols):
    return (
        lax.broadcasted_iota(jnp.int32, (rows, cols), 0),
        lax.broadcasted_iota(jnp.int32, (rows, cols), 1),
    )


def swap_matrix(orbs):
    row, col = lane_grid(orbs, orbs)
    return jnp.where(row == col + 1 - 2 * (col % 2), 1.0, 0.0).astype(BF16)


def scaled(coeff, value):
    return (coeff * value.astype(F32)).astype(BF16)


def take(refs):
    def some(count):
        return [refs.pop(0) for _ in range(count)]

    return some


def diag_kernel(
    mask_ref, hop_ref, east_ref, edge_ref, cos_ref, sin_ref,
    diag_ref, east_t_ref, east_m_ref, signed_sin_ref, cos_out_ref, *, scale
):
    cols, orbs = hop_ref.shape[0], hop_ref.shape[1]
    site, lane = lane_grid(orbs // 2, orbs)
    spread = jnp.where(site == lane // 2, coupling, 0.0)
    signed = jnp.where(lane % 2 == 0, spread, -spread)
    cosine = jnp.dot(cos_ref[...], spread, precision=HIGH, preferred_element_type=F32)
    sine = jnp.dot(sin_ref[...], spread, precision=HIGH, preferred_element_type=F32)
    sign = jnp.where(lane[:1] % 2 == 0, 1.0, -1.0)
    signed_sin_ref[...] = scale * sign * sine
    cos_out_ref[...] = scale * cosine
    cosine = sign * cosine
    row, col = lane_grid(orbs, orbs)
    on_diag = row == col
    crossed = row == col + 1 - 2 * (col % 2)
    east_m_ref[0] = edge_ref[0]
    for c in range(cols):
        hop = hop_ref[c].astype(F32)
        onsite = jnp.where(on_diag, cosine[c : c + 1], 0.0)
        onsite = jnp.where(crossed, sine[c : c + 1], onsite)
        diag_ref[c] = (hop + hop.T + onsite).astype(BF16)
        east = east_ref[c].astype(F32) * mask_ref[c].astype(F32)
        east_t_ref[c] = east.T.astype(BF16)
        if c + 1 < cols:
            east_m_ref[c + 1] = east.astype(BF16)


def vertical_kernel(side_ref, own_ref, north_ref, partner_ref, other_ref):
    def fill(south_out, north_out):
        for c in range(own_ref.shape[0]):
            south_out[c] = own_ref[c].astype(F32).T.astype(BF16)
            north_out[c] = north_ref[c]

    @pl.when(side_ref[0] == 0)
    def _():
        fill(partner_ref, other_ref)

    @pl.when(side_ref[0] != 0)
    def _():
        fill(other_ref, partner_ref)


def both(ref, c):
    block = ref[:, c]
    return block.reshape(block.shape[0] * block.shape[1], block.shape[2])


def along_row(c, block, edge_refs, ops):
    diag_ref, east_t_ref, east_m_ref = ops
    cols = diag_ref.shape[0]

    def flat(ref):
        value = ref[...]
        return value.reshape(value.shape[0] * value.shape[1], value.shape[2])

    east = block(c + 1) if c + 1 < cols else flat(edge_refs[1])
    west = block(c - 1) if c > 0 else flat(edge_refs[0])
    total = mm(block(c), diag_ref[c])
    return total + mm(east, east_t_ref[c]) + mm(west, east_m_ref[c])


def first_row_kernel(coeff_ref, *refs, width):
    some = take(list(refs))
    ops, edges, (probe_ref, left_ref) = some(3), some(2), some(2)
    outs = some(len(refs) - 7)
    cols, count = probe_ref.shape[0], probe_ref.shape[1]
    top = coeff_ref[coeff_ref.shape[0] - 1 :]

    def block(c):
        return jnp.concatenate([probe_ref[c], scaled(top, left_ref[c])], axis=0)

    edge_values = []
    for ref in edges:
        edge_values.append(jnp.concatenate([ref[0], scaled(top, ref[1])], axis=0)[None])
    blocks = [block(c) for c in range(cols)]
    for c in range(cols):
        total = along_row(c, lambda i: blocks[i], edge_values, ops)
        base = coeff_ref[3:4] * left_ref[c].astype(F32)
        outs[c // width][0, c % width] = total[:count]
        outs[c // width][1, c % width] = 2.0 * total[count:] + base


def row_kernel(coeff_ref, *refs, width, level, first):
    some = take(list(refs))
    ops, edges, (left_ref,) = some(3), some(2), some(1)
    cols = left_ref.shape[0]
    chunks = cols // width
    states = some(chunks)
    prevs = some(1) if first else some(chunks)
    outs = some(chunks)
    count = left_ref.shape[1]

    def block(c):
        return both(states[c // width], c % width)

    for c in range(cols):
        k, i = divmod(c, width)
        total = 2.0 * along_row(c, block, edges, ops)
        if first:
            old_a = prevs[0][c]
            old_g = scaled(coeff_ref[coeff_ref.shape[0] - 1 :], left_ref[c])
        else:
            old_a, old_g = prevs[k][0, i], prevs[k][1, i]
        base = coeff_ref[level : level + 1] * left_ref[c].astype(F32)
        outs[k][0, i] = total[:count] - old_a.astype(F32)
        outs[k][1, i] = total[count:] + base - old_g.astype(F32)


def column_kernel(coeff_ref, *refs, start, first):
    some = take(list(refs))
    ops, (part_ref,) = some(2), some(1)
    moved = some(4 if first else 2)
    out_ref, *edge = some(len(refs) - 3 - len(moved))
    width, count = part_ref.shape[1], part_ref.shape[2]
    top = coeff_ref[coeff_ref.shape[0] - 1 :]
    for i in range(width):
        c = start + i
        if first:
            near, far = [
                jnp.concatenate([a[c], scaled(top, g[c])], axis=0)
                for a, g in (moved[:2], moved[2:])
            ]
        else:
            near, far = both(moved[0], i), both(moved[1], i)
        total = mm(near, ops[0][c]) + mm(far, ops[1][c])
        factor = 1.0 if first else 2.0
        new_a = (part_ref[0, i] + factor * total[:count]).astype(BF16)
        new_g = (part_ref[1, i] + 2.0 * total[count:]).astype(BF16)
        out_ref[0, i] = new_a
        out_ref[1, i] = new_g
        if edge and i == (0 if start == 0 else width - 1):
            edge[0][0] = new_a
            edge[0][1] = new_g


def far_kernel(coeff_ref, *refs, width, start, done):
    some = take(list(refs))
    ops, probe_refs, left_refs, (state_ref,) = some(2), some(2), some(2), some(1)
    earlier = some(len(done))
    out_refs = some(1 if not done else 2)
    cols, _, orbs = probe_refs[0].shape
    count = state_ref.shape[2]
    top = coeff_ref[coeff_ref.shape[0] - 1 :]
    swap = swap_matrix(orbs)
    for side in range(2):
        for i in range(width):
            c = start + i
            moved = mm_t(both(state_ref, i), ops[side][c])
            moved_a, moved_g = 4.0 * moved[:count], 2.0 * moved[count:]
            p, left = probe_refs[side][c], scaled(top, left_refs[side][c])
            same = moved_g * p.astype(F32) + moved_a * left.astype(F32)
            cross = moved_g * mm(p, swap) + moved_a * mm(left, swap)
            for row, value in ((0, same), (1, cross)):
                value = jnp.sum(value, axis=0, keepdims=True)
                if done:
                    out_refs[side][row * cols + c : row * cols + c + 1, :] = value
                else:
                    at = (2 * side + row) * width + i
                    out_refs[0][at : at + 1, :] = value
        for ref, begin in zip(earlier, done):
            for row in range(2):
                at = (2 * side + row) * width
                to = row * cols + begin
                out_refs[side][to : to + width, :] = ref[at : at + width, :]


def near_kernel(coeff_ref, *refs, width):
    some = take(list(refs))
    ops, edges, (probe_ref, left_ref) = some(3), some(2), some(2)
    cols, count, orbs = probe_ref.shape
    chunks = cols // width
    first, second, third = some(chunks), some(chunks), some(chunks)
    (out_ref,) = some(1)
    top = coeff_ref[coeff_ref.shape[0] - 1 :]
    swap = swap_matrix(orbs)

    def block(c):
        return both(third[c // width], c % width)

    for c in range(cols):
        k, i = divmod(c, width)
        a = [probe_ref[c], first[k][0, i], second[k][0, i], third[k][0, i]]
        g = [third[k][1, i], second[k][1, i], first[k][1, i], scaled(top, left_ref[c])]
        total = 2.0 * along_row(c, block, edges, ops)
        last_a = total[:count] - a[2].astype(F32)
        last_g = total[count:] + coeff_ref[:1] * left_ref[c].astype(F32) - g[1].astype(F32)
        same = last_g * a[0].astype(F32)
        cross = last_g * mm(a[0], swap)
        same2 = last_a * g[3].astype(F32)
        cross2 = last_a * mm(g[3], swap)
        for n in range(3):
            same2 = same2 + g[n].astype(F32) * a[n + 1].astype(F32)
            cross2 = cross2 + g[n].astype(F32) * mm(a[n + 1], swap)
        out_ref[c : c + 1, :] = jnp.sum(same + 2.0 * same2, axis=0, keepdims=True)
        out_ref[cols + c : cols + c + 1, :] = jnp.sum(cross + 2.0 * cross2, axis=0, keepdims=True)


def torque_kernel(near_ref, partner_ref, other_ref, sin_ref, cos_ref, out_ref):
    total = near_ref[...] + partner_ref[...] + other_ref[...]
    cols, orbs = total.shape[0] // 2, total.shape[1]
    lane, site = lane_grid(orbs, orbs // 2)
    gather = jnp.where(lane // 2 == site, 1.0, 0.0)
    lanes = sin_ref[...] * total[:cols] - cos_ref[...] * total[cols:]
    out_ref[...] = jnp.dot(lanes, gather, precision=HIGH, preferred_element_type=F32)


def on_device(
    probes, left_probes, angles, cluster_hopping, east_bonds, south_bonds, bond_mask, coeffs
):
    rows, columns = (lax.axis_size("tx"), lax.axis_size("ty"))
    flip = [(i, i ^ 1) for i in range(rows)]
    onward = [(i, (i + 2) % rows if i % 2 == 0 else (i - 2) % rows) for i in range(rows)]
    outer = [(i, (i - 1) % rows if i % 2 == 0 else (i + 1) % rows) for i in range(rows)]
    south = [(i, (i + 1) % rows) for i in range(rows)]
    east = [(i, (i + 1) % columns) for i in range(columns)]
    west = [(j, i) for i, j in east]
    side = (lax.axis_index("tx") % 2).astype(jnp.int32).reshape(1)

    probes, left, angles = probes[0], left_probes[0], angles[0]
    hop, ebond, sbond = cluster_hopping[0], east_bonds[0], south_bonds[0]
    cols, count, orbs = probes.shape
    width = cols // CHUNKS
    order = [0, CHUNKS - 1, *range(1, CHUNKS - 1)]
    unit = 4 * count * orbs * orbs

    near_p = lax.ppermute(probes, "tx", flip)
    near_l = lax.ppermute(left, "tx", flip)
    probes_later, left_later, ebond, coeffs, _ = lax.optimization_barrier(
        (probes, left, ebond, coeffs, near_p)
    )
    coeffs = jnp.broadcast_to(coeffs[:, None], (coeffs.shape[0], orbs))
    east_edge = jnp.stack([probes_later[cols - 1], left_later[cols - 1]])
    west_edge = jnp.stack([probes_later[0], left_later[0]])
    edges = (lax.ppermute(east_edge, "ty", east), lax.ppermute(west_edge, "ty", west))
    far_p = lax.ppermute(near_p, "tx", onward)
    south_own = jnp.where(bond_mask[1, 0][:, None, None] != 0, sbond, jnp.zeros_like(sbond))
    south_send, _ = lax.optimization_barrier((south_own, near_l))
    south_in = lax.ppermute(south_send, "tx", south)
    far_l = lax.ppermute(near_l, "tx", onward)
    last_bond = jnp.where(bond_mask[0, 0, cols - 1] != 0, ebond[cols - 1 :], 0).astype(BF16)
    east_in = lax.ppermute(last_bond, "ty", east)

    big = sds((cols, orbs, orbs), BF16)
    lanes = sds((cols, orbs), F32)

    def build(*refs):
        diag_kernel(*refs, scale=1.0 / count)

    diag, east_t, east_m, sine, cosine = call(
        build, (big, big, big, lanes, lanes),
        bond_mask[0, 0], hop, ebond, east_in, jnp.cos(angles), jnp.sin(angles), scalars=1,
    )
    near_m, far_m = call(vertical_kernel, (big, big), side, south_own, south_in, scalars=1)
    ops = (diag, east_t, east_m)
    part = sds((2, width, count, orbs), F32)
    state = sds((2, width, count, orbs), BF16)
    edge = sds((2, count, orbs), BF16)

    def across(parts, moved, first):
        out, ends = [None] * CHUNKS, {}
        for k in order:
            start = k * width

            def body(*refs, start=start):
                column_kernel(*refs, start=start, first=first)

            shapes = (state, edge) if k in (0, CHUNKS - 1) else (state,)
            out[k], *more = call(
                body, shapes, coeffs, near_m, far_m, parts[k], *moved[k], flops=2 * width * unit
            )
            if more:
                ends[k] = more[0]
        return out, ends[0], ends[CHUNKS - 1]

    def first_row(*refs):
        first_row_kernel(*refs, width=width)

    parts = call(
        first_row, (part,) * CHUNKS, coeffs, *ops, *edges, probes, left, flops=3 * cols * unit
    )
    now, low, high = across(parts, [(near_p, near_l, far_p, far_l)] * CHUNKS, True)
    states = [now]
    for n in (1, 2):
        near, far = [None] * CHUNKS, [None] * CHUNKS
        edges = (lax.ppermute(high, "ty", east), lax.ppermute(low, "ty", west))
        now[order[2]], *edges = lax.optimization_barrier((now[order[2]], *edges))
        for k in order:
            near[k] = lax.ppermute(now[k], "tx", flip)
        for k in order:
            far[k] = lax.ppermute(near[k], "tx", onward)

        def body(*refs, n=n):
            row_kernel(*refs, width=width, level=3 - n, first=n == 1)

        prev = [probes] if n == 1 else states[-2]
        parts = call(
            body, (part,) * CHUNKS, coeffs, *ops, *edges, left, *now, *prev,
            flops=3 * cols * unit,
        )
        now, low, high = across(parts, list(zip(near, far)), False)
        states.append(now)

    edges = (lax.ppermute(high, "ty", east), lax.ppermute(low, "ty", west))
    sums = sds((2 * cols, orbs), F32)

    pieces = []
    for k in order:
        done = [j * width for j in order[:-1]] if k == order[-1] else []

        def far_sums(*refs, start=k * width, done=done):
            far_kernel(*refs, width=width, start=start, done=done)

        shapes = (sums, sums) if done else (sds((4 * width, orbs), F32),)
        pieces += call(
            far_sums, shapes, coeffs, near_m, far_m, near_p, far_p, near_l, far_l, now[k],
            *(pieces if done else []), flops=4 * width * unit,
        )
    to_partner, to_other = pieces[-2:]

    def near_sums(*refs):
        near_kernel(*refs, width=width)

    from_other = lax.ppermute(to_other, "tx", outer)
    from_partner = lax.ppermute(to_partner, "tx", flip)
    (own,) = call(
        near_sums, (sums,), coeffs, *ops, *edges, probes, left, *states[0], *states[1], *now,
        flops=6 * cols * unit,
    )
    (torque,) = call(
        torque_kernel, (sds((cols, orbs // 2), F32),),
        own, from_partner, from_other, sine, cosine,
    )
    return torque[None]


def solution(mesh):
    placed = (
        P("tx", "ty", None, None),
        P("tx", "ty", None, None),
        P("tx", "ty", None),
        P("tx", "ty", None, None),
        P("tx", "ty", None, None),
        P("tx", "ty", None, None),
        P(None, "tx", "ty"),
        P(),
    )
    return jax.shard_map(
        on_device, mesh=mesh, in_specs=placed, out_specs=P("tx", "ty", None), check_vma=False
    )
```

```python
import jax
import jax.numpy as jnp
from jax import lax
from jax.experimental import pallas as pl
from jax.experimental.pallas import tpu as pltpu
from jax.sharding import PartitionSpec as P

coupling = 0.5
EIGHTHS = (2, 2, 2, 2)
F32 = jnp.float32
BF16 = jnp.bfloat16
VM = pl.BlockSpec(memory_space=pltpu.VMEM)
SM = pl.BlockSpec(memory_space=pltpu.SMEM)
HIGH = lax.Precision.HIGHEST


def mm(x, y):
    return lax.dot_general(x, y, (((1,), (0,)), ((), ())), preferred_element_type=F32)


def mm_t(x, y):
    return lax.dot_general(x, y, (((1,), (1,)), ((), ())), preferred_element_type=F32)


def sds(shape, dtype):
    return jax.ShapeDtypeStruct(tuple(shape), dtype)


def call(body, outs, *args, scalars=0, flops=0):
    nbytes = sum(a.size * a.dtype.itemsize for a in (*args, *outs))
    return pl.pallas_call(
        body,
        out_shape=tuple(outs),
        in_specs=[SM] * scalars + [VM] * (len(args) - scalars),
        out_specs=tuple(VM for _ in outs),
        cost_estimate=pl.CostEstimate(flops=flops, transcendentals=0, bytes_accessed=nbytes),
        compiler_params=pltpu.CompilerParams(vmem_limit_bytes=32 * 1024 * 1024),
    )(*args)


def lane_grid(rows, cols):
    return (
        lax.broadcasted_iota(jnp.int32, (rows, cols), 0),
        lax.broadcasted_iota(jnp.int32, (rows, cols), 1),
    )


def swap_matrix(orbs):
    row, col = lane_grid(orbs, orbs)
    return jnp.where(row == col + 1 - 2 * (col % 2), 1.0, 0.0).astype(BF16)


def scaled(coeff, value):
    return (coeff * value.astype(F32)).astype(BF16)


def places(widths):
    return [(k, i) for k, width in enumerate(widths) for i in range(width)]


def take(refs):
    def some(count):
        return [refs.pop(0) for _ in range(count)]

    return some


def diag_kernel(
    mask_ref, hop_ref, east_ref, edge_ref, cos_ref, sin_ref,
    diag_ref, east_t_ref, east_m_ref, signed_sin_ref, cos_out_ref, *, scale
):
    cols, orbs = hop_ref.shape[0], hop_ref.shape[1]
    site, lane = lane_grid(orbs // 2, orbs)
    spread = jnp.where(site == lane // 2, coupling, 0.0)
    signed = jnp.where(lane % 2 == 0, spread, -spread)
    cosine = jnp.dot(cos_ref[...], spread, precision=HIGH, preferred_element_type=F32)
    sine = jnp.dot(sin_ref[...], spread, precision=HIGH, preferred_element_type=F32)
    sign = jnp.where(lane[:1] % 2 == 0, 1.0, -1.0)
    signed_sin_ref[...] = scale * sign * sine
    cos_out_ref[...] = scale * cosine
    cosine = sign * cosine
    row, col = lane_grid(orbs, orbs)
    on_diag = row == col
    crossed = row == col + 1 - 2 * (col % 2)
    east_m_ref[0] = edge_ref[0]
    for c in range(cols):
        hop = hop_ref[c].astype(F32)
        onsite = jnp.where(on_diag, cosine[c : c + 1], 0.0)
        onsite = jnp.where(crossed, sine[c : c + 1], onsite)
        diag_ref[c] = (hop + hop.T + onsite).astype(BF16)
        east = east_ref[c].astype(F32) * mask_ref[c].astype(F32)
        east_t_ref[c] = east.T.astype(BF16)
        if c + 1 < cols:
            east_m_ref[c + 1] = east.astype(BF16)


def vertical_kernel(side_ref, *refs):
    *given, partner_ref, other_ref = refs
    pieces = len(given) // 2
    size = given[0].shape[0]

    def fill(south_out, north_out):
        for n, (own_ref, north_ref) in enumerate(zip(given[:pieces], given[pieces:])):
            for c in range(size):
                south_out[n * size + c] = own_ref[c].astype(F32).T.astype(BF16)
                north_out[n * size + c] = north_ref[c]

    @pl.when(side_ref[0] == 0)
    def _():
        fill(partner_ref, other_ref)

    @pl.when(side_ref[0] != 0)
    def _():
        fill(other_ref, partner_ref)


def both(ref, c):
    block = ref[:, c]
    return block.reshape(block.shape[0] * block.shape[1], block.shape[2])


def along_row(c, block, edge_refs, ops):
    diag_ref, east_t_ref, east_m_ref = ops
    cols = diag_ref.shape[0]

    def flat(ref):
        value = ref[...]
        return value.reshape(value.shape[0] * value.shape[1], value.shape[2])

    east = block(c + 1) if c + 1 < cols else flat(edge_refs[1])
    west = block(c - 1) if c > 0 else flat(edge_refs[0])
    total = mm(block(c), diag_ref[c])
    return total + mm(east, east_t_ref[c]) + mm(west, east_m_ref[c])


def first_row_kernel(coeff_ref, *refs, spots):
    some = take(list(refs))
    ops, edges, (probe_ref, left_ref) = some(3), some(2), some(2)
    outs = some(len(refs) - 7)
    cols, count = probe_ref.shape[0], probe_ref.shape[1]
    top = coeff_ref[coeff_ref.shape[0] - 1 :]

    def block(c):
        return jnp.concatenate([probe_ref[c], scaled(top, left_ref[c])], axis=0)

    edge_values = []
    for ref in edges:
        edge_values.append(jnp.concatenate([ref[0], scaled(top, ref[1])], axis=0)[None])
    blocks = [block(c) for c in range(cols)]
    for c in range(cols):
        total = along_row(c, lambda i: blocks[i], edge_values, ops)
        base = coeff_ref[3:4] * left_ref[c].astype(F32)
        k, i = spots[c]
        outs[k][0, i] = total[:count]
        outs[k][1, i] = 2.0 * total[count:] + base


def row_kernel(coeff_ref, *refs, spots, level, first):
    some = take(list(refs))
    ops, edges, (left_ref,) = some(3), some(2), some(1)
    cols = left_ref.shape[0]
    chunks = spots[-1][0] + 1
    states = some(chunks)
    prevs = some(1) if first else some(chunks)
    outs = some(chunks)
    count = left_ref.shape[1]

    def block(c):
        return both(states[spots[c][0]], spots[c][1])

    for c in range(cols):
        k, i = spots[c]
        total = 2.0 * along_row(c, block, edges, ops)
        if first:
            old_a = prevs[0][c]
            old_g = scaled(coeff_ref[coeff_ref.shape[0] - 1 :], left_ref[c])
        else:
            old_a, old_g = prevs[k][0, i], prevs[k][1, i]
        base = coeff_ref[level : level + 1] * left_ref[c].astype(F32)
        outs[k][0, i] = total[:count] - old_a.astype(F32)
        outs[k][1, i] = total[count:] + base - old_g.astype(F32)


def column_kernel(coeff_ref, *refs, start, first):
    some = take(list(refs))
    ops, (part_ref,) = some(2), some(1)
    moved = some(4 if first else 2)
    out_ref, *edge = some(len(refs) - 3 - len(moved))
    width, count = part_ref.shape[1], part_ref.shape[2]
    top = coeff_ref[coeff_ref.shape[0] - 1 :]
    for i in range(width):
        c = start + i
        if first:
            near, far = [
                jnp.concatenate([a[c], scaled(top, g[c])], axis=0)
                for a, g in (moved[:2], moved[2:])
            ]
        else:
            near, far = both(moved[0], i), both(moved[1], i)
        total = mm(near, ops[0][c]) + mm(far, ops[1][c])
        factor = 1.0 if first else 2.0
        new_a = (part_ref[0, i] + factor * total[:count]).astype(BF16)
        new_g = (part_ref[1, i] + 2.0 * total[count:]).astype(BF16)
        out_ref[0, i] = new_a
        out_ref[1, i] = new_g
        if edge and i == (0 if start == 0 else width - 1):
            edge[0][0] = new_a
            edge[0][1] = new_g


def far_kernel(coeff_ref, *refs, start, done):
    some = take(list(refs))
    ops, probe_refs, left_refs, (state_ref,) = some(2), some(2), some(2), some(1)
    earlier = some(len(done))
    out_refs = some(1 if not done else 2)
    cols, _, orbs = probe_refs[0].shape
    width, count = state_ref.shape[1], state_ref.shape[2]
    top = coeff_ref[coeff_ref.shape[0] - 1 :]
    swap = swap_matrix(orbs)
    for side in range(2):
        for i in range(width):
            c = start + i
            moved = mm_t(both(state_ref, i), ops[side][c])
            moved_a, moved_g = 4.0 * moved[:count], 2.0 * moved[count:]
            p, left = probe_refs[side][c], scaled(top, left_refs[side][c])
            same = moved_g * p.astype(F32) + moved_a * left.astype(F32)
            cross = moved_g * mm(p, swap) + moved_a * mm(left, swap)
            for row, value in ((0, same), (1, cross)):
                value = jnp.sum(value, axis=0, keepdims=True)
                if done:
                    out_refs[side][row * cols + c : row * cols + c + 1, :] = value
                else:
                    at = (2 * side + row) * width + i
                    out_refs[0][at : at + 1, :] = value
        for ref, begin in zip(earlier, done):
            size = ref.shape[0] // 4
            for row in range(2):
                at = (2 * side + row) * size
                to = row * cols + begin
                out_refs[side][to : to + size, :] = ref[at : at + size, :]


def near_kernel(coeff_ref, *refs, spots):
    some = take(list(refs))
    ops, edges, (probe_ref, left_ref) = some(3), some(2), some(2)
    cols, count, orbs = probe_ref.shape
    chunks = spots[-1][0] + 1
    first, second, third = some(chunks), some(chunks), some(chunks)
    (out_ref,) = some(1)
    top = coeff_ref[coeff_ref.shape[0] - 1 :]
    swap = swap_matrix(orbs)

    def block(c):
        return both(third[spots[c][0]], spots[c][1])

    for c in range(cols):
        k, i = spots[c]
        a = [probe_ref[c], first[k][0, i], second[k][0, i], third[k][0, i]]
        g = [third[k][1, i], second[k][1, i], first[k][1, i], scaled(top, left_ref[c])]
        total = 2.0 * along_row(c, block, edges, ops)
        last_a = total[:count] - a[2].astype(F32)
        last_g = total[count:] + coeff_ref[:1] * left_ref[c].astype(F32) - g[1].astype(F32)
        same = last_g * a[0].astype(F32)
        cross = last_g * mm(a[0], swap)
        same2 = last_a * g[3].astype(F32)
        cross2 = last_a * mm(g[3], swap)
        for n in range(3):
            same2 = same2 + g[n].astype(F32) * a[n + 1].astype(F32)
            cross2 = cross2 + g[n].astype(F32) * mm(a[n + 1], swap)
        out_ref[c : c + 1, :] = jnp.sum(same + 2.0 * same2, axis=0, keepdims=True)
        out_ref[cols + c : cols + c + 1, :] = jnp.sum(cross + 2.0 * cross2, axis=0, keepdims=True)


def torque_kernel(near_ref, partner_ref, other_ref, sin_ref, cos_ref, out_ref):
    total = near_ref[...] + partner_ref[...] + other_ref[...]
    cols, orbs = total.shape[0] // 2, total.shape[1]
    lane, site = lane_grid(orbs, orbs // 2)
    gather = jnp.where(lane // 2 == site, 1.0, 0.0)
    lanes = sin_ref[...] * total[:cols] - cos_ref[...] * total[cols:]
    out_ref[...] = jnp.dot(lanes, gather, precision=HIGH, preferred_element_type=F32)


def on_device(
    probes, left_probes, angles, cluster_hopping, east_bonds, south_bonds, bond_mask, coeffs
):
    rows, columns = (lax.axis_size("tx"), lax.axis_size("ty"))
    flip = [(i, i ^ 1) for i in range(rows)]
    onward = [(i, (i + 2) % rows if i % 2 == 0 else (i - 2) % rows) for i in range(rows)]
    outer = [(i, (i - 1) % rows if i % 2 == 0 else (i + 1) % rows) for i in range(rows)]
    south = [(i, (i + 1) % rows) for i in range(rows)]
    east = [(i, (i + 1) % columns) for i in range(columns)]
    west = [(j, i) for i, j in east]
    side = (lax.axis_index("tx") % 2).astype(jnp.int32).reshape(1)

    probes, left, angles = probes[0], left_probes[0], angles[0]
    hop, ebond, sbond = cluster_hopping[0], east_bonds[0], south_bonds[0]
    cols, count, orbs = probes.shape
    widths = [cols * part // 8 for part in EIGHTHS]
    chunks = len(widths)
    starts = [sum(widths[:k]) for k in range(chunks)]
    spots = places(widths)
    order = [0, chunks - 1, *range(1, chunks - 1)]
    unit = 4 * count * orbs * orbs
    half = cols // 2

    odd = lax.axis_index("tx") % 2 == 1
    near_p = lax.ppermute(probes, "tx", flip)
    near_l = lax.ppermute(left, "tx", flip)
    far_p = lax.ppermute(near_p, "tx", onward)
    far_l = lax.ppermute(near_l, "tx", onward)
    later = (probes, left, ebond, coeffs)
    *later, _ = lax.optimization_barrier((*later, near_p))
    probes_later, left_later, ebond, coeffs = later
    present = bond_mask[1, 0][:, None, None] != 0
    south_own = [
        jnp.where(present[part], sbond[part], jnp.zeros_like(sbond[part]))
        for part in (slice(0, half), slice(half, cols))
    ]
    stepped = lax.ppermute(south_own[1], "tx", [(i, (i + 2) % rows) for i in range(1, rows, 2)])
    crossing = jnp.where(odd, stepped, south_own[1])
    south_in = [lax.ppermute(south_own[0], "tx", south), lax.ppermute(crossing, "tx", flip)]
    coeffs = jnp.broadcast_to(coeffs[:, None], (coeffs.shape[0], orbs))
    east_edge = jnp.stack([probes_later[cols - 1], left_later[cols - 1]])
    west_edge = jnp.stack([probes_later[0], left_later[0]])
    edges = (lax.ppermute(east_edge, "ty", east), lax.ppermute(west_edge, "ty", west))
    last_bond = jnp.where(bond_mask[0, 0, cols - 1] != 0, ebond[cols - 1 :], 0).astype(BF16)
    east_in = lax.ppermute(last_bond, "ty", east)

    big = sds((cols, orbs, orbs), BF16)
    lanes = sds((cols, orbs), F32)

    def build(*refs):
        diag_kernel(*refs, scale=1.0 / count)

    diag, east_t, east_m, sine, cosine = call(
        build, (big, big, big, lanes, lanes),
        bond_mask[0, 0], hop, ebond, east_in, jnp.cos(angles), jnp.sin(angles), scalars=1,
    )
    near_m, far_m = call(
        vertical_kernel, (big, big), side, *south_own, *south_in, scalars=1
    )
    ops = (diag, east_t, east_m)
    part = [sds((2, width, count, orbs), F32) for width in widths]
    state = [sds((2, width, count, orbs), BF16) for width in widths]
    edge = sds((2, count, orbs), BF16)

    def across(k, parts, moved, first):
        def body(*refs):
            column_kernel(*refs, start=starts[k], first=first)

        shapes = (state[k], edge) if k in (0, chunks - 1) else (state[k],)
        return call(
            body, shapes, coeffs, near_m, far_m, parts[k], *moved, flops=2 * widths[k] * unit
        )

    def first_row(*refs):
        first_row_kernel(*refs, spots=spots)

    parts = call(
        first_row, part, coeffs, *ops, *edges, probes, left, flops=3 * cols * unit
    )
    made = {k: across(k, parts, (near_p, near_l, far_p, far_l), True) for k in order}
    states = []

    def row_parts(n, now, prev, edges):
        def body(*refs):
            row_kernel(*refs, spots=spots, level=3 - n, first=n == 1)

        return call(
            body, part, coeffs, *ops, *edges, left, *now, *prev, flops=3 * cols * unit
        )

    for n in (1, 2):
        now = [made[k][0] for k in range(chunks)]
        low, high = made[0][1], made[chunks - 1][1]
        states.append(now)
        near, far = [None] * chunks, [None] * chunks
        edges = (lax.ppermute(high, "ty", east), lax.ppermute(low, "ty", west))
        for j, k in enumerate(order):
            if j == 2:
                now[k], *edges = lax.optimization_barrier((now[k], *edges))
            near[k] = lax.ppermute(now[k], "tx", flip)
        prev = [probes] if n == 1 else states[-2]
        made = {}
        for j, k in enumerate(order):
            send = near[k]
            if j == 0:
                send, *edges = lax.optimization_barrier((send, *edges))
            if j == chunks - 1:
                send, first, *more = lax.optimization_barrier((send, *made[order[0]]))
                made[order[0]] = [first, *more]
            far[k] = lax.ppermute(send, "tx", onward)
            if j == 0:
                parts = row_parts(n, now, prev, edges)
            if j >= chunks - 2:
                for i in order[: j + 1]:
                    if i not in made:
                        made[i] = across(i, parts, (near[i], far[i]), False)

    now = [made[k][0] for k in range(chunks)]
    low, high = made[0][1], made[chunks - 1][1]
    states.append(now)
    low, high = lax.optimization_barrier((low, high))
    edges = (lax.ppermute(high, "ty", east), lax.ppermute(low, "ty", west))
    sums = sds((2 * cols, orbs), F32)

    pieces = []
    for k in order:
        done = [starts[j] for j in order[:-1]] if k == order[-1] else []

        def far_sums(*refs, start=starts[k], done=done):
            far_kernel(*refs, start=start, done=done)

        shapes = (sums, sums) if done else (sds((4 * widths[k], orbs), F32),)
        pieces += call(
            far_sums, shapes, coeffs, near_m, far_m, near_p, far_p, near_l, far_l, now[k],
            *(pieces if done else []), flops=4 * widths[k] * unit,
        )
    to_partner, to_other = pieces[-2:]

    def near_sums(*refs):
        near_kernel(*refs, spots=spots)

    from_other = lax.ppermute(to_other, "tx", outer)
    from_partner = lax.ppermute(to_partner, "tx", flip)
    (own,) = call(
        near_sums, (sums,), coeffs, *ops, *edges, probes, left, *states[0], *states[1], *now,
        flops=6 * cols * unit,
    )
    (torque,) = call(
        torque_kernel, (sds((cols, orbs // 2), F32),),
        own, from_partner, from_other, sine, cosine,
    )
    return torque[None]


def solution(mesh):
    placed = (
        P("tx", "ty", None, None),
        P("tx", "ty", None, None),
        P("tx", "ty", None),
        P("tx", "ty", None, None),
        P("tx", "ty", None, None),
        P("tx", "ty", None, None),
        P(None, "tx", "ty"),
        P(),
    )
    return jax.shard_map(
        on_device, mesh=mesh, in_specs=placed, out_specs=P("tx", "ty", None), check_vma=False
    )
```

```python
import jax
import jax.numpy as jnp
from jax import lax
from jax.experimental import pallas as pl
from jax.experimental.pallas import tpu as pltpu
from jax.sharding import PartitionSpec as P

coupling = 0.5
EIGHTHS = (2, 2, 2, 2)
F32 = jnp.float32
BF16 = jnp.bfloat16
VM = pl.BlockSpec(memory_space=pltpu.VMEM)
SM = pl.BlockSpec(memory_space=pltpu.SMEM)
HIGH = lax.Precision.HIGHEST


def mm(x, y):
    return lax.dot_general(x, y, (((1,), (0,)), ((), ())), preferred_element_type=F32)


def mm_t(x, y):
    return lax.dot_general(x, y, (((1,), (1,)), ((), ())), preferred_element_type=F32)


def sds(shape, dtype):
    return jax.ShapeDtypeStruct(tuple(shape), dtype)


def call(body, outs, *args, scalars=0, flops=0):
    nbytes = sum(a.size * a.dtype.itemsize for a in (*args, *outs))
    return pl.pallas_call(
        body,
        out_shape=tuple(outs),
        in_specs=[SM] * scalars + [VM] * (len(args) - scalars),
        out_specs=tuple(VM for _ in outs),
        cost_estimate=pl.CostEstimate(flops=flops, transcendentals=0, bytes_accessed=nbytes),
        compiler_params=pltpu.CompilerParams(vmem_limit_bytes=32 * 1024 * 1024),
    )(*args)


def lane_grid(rows, cols):
    return (
        lax.broadcasted_iota(jnp.int32, (rows, cols), 0),
        lax.broadcasted_iota(jnp.int32, (rows, cols), 1),
    )


def swap_matrix(orbs):
    row, col = lane_grid(orbs, orbs)
    return jnp.where(row == col + 1 - 2 * (col % 2), 1.0, 0.0).astype(BF16)


def scaled(coeff, value):
    return (coeff * value.astype(F32)).astype(BF16)


def places(widths):
    return [(k, i) for k, width in enumerate(widths) for i in range(width)]


def take(refs):
    def some(count):
        return [refs.pop(0) for _ in range(count)]

    return some


def diag_kernel(
    mask_ref, hop_ref, east_ref, edge_ref, cos_ref, sin_ref,
    diag_ref, east_t_ref, east_m_ref, signed_sin_ref, cos_out_ref, *, scale
):
    cols, orbs = hop_ref.shape[0], hop_ref.shape[1]
    site, lane = lane_grid(orbs // 2, orbs)
    spread = jnp.where(site == lane // 2, coupling, 0.0)
    signed = jnp.where(lane % 2 == 0, spread, -spread)
    cosine = jnp.dot(cos_ref[...], spread, precision=HIGH, preferred_element_type=F32)
    sine = jnp.dot(sin_ref[...], spread, precision=HIGH, preferred_element_type=F32)
    sign = jnp.where(lane[:1] % 2 == 0, 1.0, -1.0)
    signed_sin_ref[...] = scale * sign * sine
    cos_out_ref[...] = scale * cosine
    cosine = sign * cosine
    row, col = lane_grid(orbs, orbs)
    on_diag = row == col
    crossed = row == col + 1 - 2 * (col % 2)
    east_m_ref[0] = edge_ref[0]
    for c in range(cols):
        hop = hop_ref[c].astype(F32)
        onsite = jnp.where(on_diag, cosine[c : c + 1], 0.0)
        onsite = jnp.where(crossed, sine[c : c + 1], onsite)
        diag_ref[c] = (hop + hop.T + onsite).astype(BF16)
        east = east_ref[c].astype(F32) * mask_ref[c].astype(F32)
        east_t_ref[c] = east.T.astype(BF16)
        if c + 1 < cols:
            east_m_ref[c + 1] = east.astype(BF16)


def vertical_kernel(
    side_ref, own_lo, own_hi, lo_even, lo_odd, hi_north, partner_ref, other_ref
):
    half = own_lo.shape[0]

    def fill(south_out, north_out, lo_north):
        for begin, own_ref, north_ref in ((0, own_lo, lo_north), (half, own_hi, hi_north)):
            for c in range(half):
                south_out[begin + c] = own_ref[c].astype(F32).T.astype(BF16)
                north_out[begin + c] = north_ref[c]

    @pl.when(side_ref[0] == 0)
    def _():
        fill(partner_ref, other_ref, lo_even)

    @pl.when(side_ref[0] != 0)
    def _():
        fill(other_ref, partner_ref, lo_odd)


def both(ref, c):
    block = ref[:, c]
    return block.reshape(block.shape[0] * block.shape[1], block.shape[2])


def along_row(c, block, edge_refs, ops):
    diag_ref, east_t_ref, east_m_ref = ops
    cols = diag_ref.shape[0]

    def flat(ref):
        value = ref[...]
        return value.reshape(value.shape[0] * value.shape[1], value.shape[2])

    east = block(c + 1) if c + 1 < cols else flat(edge_refs[1])
    west = block(c - 1) if c > 0 else flat(edge_refs[0])
    total = mm(block(c), diag_ref[c])
    return total + mm(east, east_t_ref[c]) + mm(west, east_m_ref[c])


def first_row_kernel(coeff_ref, *refs, spots):
    some = take(list(refs))
    ops, edges, (probe_ref, left_ref) = some(3), some(2), some(2)
    outs = some(len(refs) - 7)
    cols, count = probe_ref.shape[0], probe_ref.shape[1]
    top = coeff_ref[coeff_ref.shape[0] - 1 :]

    def block(c):
        return jnp.concatenate([probe_ref[c], scaled(top, left_ref[c])], axis=0)

    edge_values = []
    for ref in edges:
        edge_values.append(jnp.concatenate([ref[0], scaled(top, ref[1])], axis=0)[None])
    blocks = [block(c) for c in range(cols)]
    for c in range(cols):
        total = along_row(c, lambda i: blocks[i], edge_values, ops)
        base = coeff_ref[3:4] * left_ref[c].astype(F32)
        k, i = spots[c]
        outs[k][0, i] = total[:count]
        outs[k][1, i] = 2.0 * total[count:] + base


def row_kernel(coeff_ref, *refs, spots, level, first):
    some = take(list(refs))
    ops, edges, (left_ref,) = some(3), some(2), some(1)
    cols = left_ref.shape[0]
    chunks = spots[-1][0] + 1
    states = some(chunks)
    prevs = some(1) if first else some(chunks)
    outs = some(chunks)
    count = left_ref.shape[1]

    def block(c):
        return both(states[spots[c][0]], spots[c][1])

    for c in range(cols):
        k, i = spots[c]
        total = 2.0 * along_row(c, block, edges, ops)
        if first:
            old_a = prevs[0][c]
            old_g = scaled(coeff_ref[coeff_ref.shape[0] - 1 :], left_ref[c])
        else:
            old_a, old_g = prevs[k][0, i], prevs[k][1, i]
        base = coeff_ref[level : level + 1] * left_ref[c].astype(F32)
        outs[k][0, i] = total[:count] - old_a.astype(F32)
        outs[k][1, i] = total[count:] + base - old_g.astype(F32)


def column_kernel(coeff_ref, *refs, start, first):
    some = take(list(refs))
    ops, (part_ref,) = some(2), some(1)
    moved = some(4 if first else 2)
    out_ref, *edge = some(len(refs) - 3 - len(moved))
    width, count = part_ref.shape[1], part_ref.shape[2]
    top = coeff_ref[coeff_ref.shape[0] - 1 :]
    for i in range(width):
        c = start + i
        if first:
            near, far = [
                jnp.concatenate([a[c], scaled(top, g[c])], axis=0)
                for a, g in (moved[:2], moved[2:])
            ]
        else:
            near, far = both(moved[0], i), both(moved[1], i)
        total = mm(near, ops[0][c]) + mm(far, ops[1][c])
        factor = 1.0 if first else 2.0
        new_a = (part_ref[0, i] + factor * total[:count]).astype(BF16)
        new_g = (part_ref[1, i] + 2.0 * total[count:]).astype(BF16)
        out_ref[0, i] = new_a
        out_ref[1, i] = new_g
        if edge and i == (0 if start == 0 else width - 1):
            edge[0][0] = new_a
            edge[0][1] = new_g


def far_kernel(coeff_ref, *refs, start, done):
    some = take(list(refs))
    ops, probe_refs, left_refs, (state_ref,) = some(2), some(2), some(2), some(1)
    earlier = some(len(done))
    out_refs = some(1 if not done else 2)
    cols, _, orbs = probe_refs[0].shape
    width, count = state_ref.shape[1], state_ref.shape[2]
    top = coeff_ref[coeff_ref.shape[0] - 1 :]
    swap = swap_matrix(orbs)
    for side in range(2):
        for i in range(width):
            c = start + i
            moved = mm_t(both(state_ref, i), ops[side][c])
            moved_a, moved_g = 4.0 * moved[:count], 2.0 * moved[count:]
            p, left = probe_refs[side][c], scaled(top, left_refs[side][c])
            same = moved_g * p.astype(F32) + moved_a * left.astype(F32)
            cross = moved_g * mm(p, swap) + moved_a * mm(left, swap)
            for row, value in ((0, same), (1, cross)):
                value = jnp.sum(value, axis=0, keepdims=True)
                if done:
                    out_refs[side][row * cols + c : row * cols + c + 1, :] = value
                else:
                    at = (2 * side + row) * width + i
                    out_refs[0][at : at + 1, :] = value
        for ref, begin in zip(earlier, done):
            size = ref.shape[0] // 4
            for row in range(2):
                at = (2 * side + row) * size
                to = row * cols + begin
                out_refs[side][to : to + size, :] = ref[at : at + size, :]


def near_kernel(coeff_ref, *refs, spots):
    some = take(list(refs))
    ops, edges, (probe_ref, left_ref) = some(3), some(2), some(2)
    cols, count, orbs = probe_ref.shape
    chunks = spots[-1][0] + 1
    first, second, third = some(chunks), some(chunks), some(chunks)
    (out_ref,) = some(1)
    top = coeff_ref[coeff_ref.shape[0] - 1 :]
    swap = swap_matrix(orbs)

    def block(c):
        return both(third[spots[c][0]], spots[c][1])

    for c in range(cols):
        k, i = spots[c]
        a = [probe_ref[c], first[k][0, i], second[k][0, i], third[k][0, i]]
        g = [third[k][1, i], second[k][1, i], first[k][1, i], scaled(top, left_ref[c])]
        total = 2.0 * along_row(c, block, edges, ops)
        last_a = total[:count] - a[2].astype(F32)
        last_g = total[count:] + coeff_ref[:1] * left_ref[c].astype(F32) - g[1].astype(F32)
        same = last_g * a[0].astype(F32)
        cross = last_g * mm(a[0], swap)
        same2 = last_a * g[3].astype(F32)
        cross2 = last_a * mm(g[3], swap)
        for n in range(3):
            same2 = same2 + g[n].astype(F32) * a[n + 1].astype(F32)
            cross2 = cross2 + g[n].astype(F32) * mm(a[n + 1], swap)
        out_ref[c : c + 1, :] = jnp.sum(same + 2.0 * same2, axis=0, keepdims=True)
        out_ref[cols + c : cols + c + 1, :] = jnp.sum(cross + 2.0 * cross2, axis=0, keepdims=True)


def torque_kernel(near_ref, partner_ref, other_ref, sin_ref, cos_ref, out_ref):
    total = near_ref[...] + partner_ref[...] + other_ref[...]
    cols, orbs = total.shape[0] // 2, total.shape[1]
    lane, site = lane_grid(orbs, orbs // 2)
    gather = jnp.where(lane // 2 == site, 1.0, 0.0)
    lanes = sin_ref[...] * total[:cols] - cos_ref[...] * total[cols:]
    out_ref[...] = jnp.dot(lanes, gather, precision=HIGH, preferred_element_type=F32)


def on_device(
    probes, left_probes, angles, cluster_hopping, east_bonds, south_bonds, bond_mask, coeffs
):
    rows, columns = (lax.axis_size("tx"), lax.axis_size("ty"))
    flip = [(i, i ^ 1) for i in range(rows)]
    onward = [(i, (i + 2) % rows if i % 2 == 0 else (i - 2) % rows) for i in range(rows)]
    outer = [(i, (i - 1) % rows if i % 2 == 0 else (i + 1) % rows) for i in range(rows)]
    south = [(i, (i + 1) % rows) for i in range(rows)]
    east = [(i, (i + 1) % columns) for i in range(columns)]
    west = [(j, i) for i, j in east]
    side = (lax.axis_index("tx") % 2).astype(jnp.int32).reshape(1)

    probes, left, angles = probes[0], left_probes[0], angles[0]
    hop, ebond, sbond = cluster_hopping[0], east_bonds[0], south_bonds[0]
    cols, count, orbs = probes.shape
    widths = [cols * part // 8 for part in EIGHTHS]
    chunks = len(widths)
    starts = [sum(widths[:k]) for k in range(chunks)]
    spots = places(widths)
    order = [0, chunks - 1, *range(1, chunks - 1)]
    unit = 4 * count * orbs * orbs
    half = cols // 2

    odd = lax.axis_index("tx") % 2 == 1
    near_p = lax.ppermute(probes, "tx", flip)
    far_p = lax.ppermute(near_p, "tx", onward)
    present = bond_mask[1, 0][:, None, None] != 0
    south_lo, south_hi = [
        jnp.where(present[part], sbond[part], jnp.zeros_like(sbond[part]))
        for part in (slice(0, half), slice(half, cols))
    ]
    stepped = lax.ppermute(south_hi, "tx", [(i, (i + 2) % rows) for i in range(1, rows, 2)])
    lo_odd = lax.ppermute(south_lo, "tx", flip)
    lo_even = lax.ppermute(lo_odd, "tx", [(i, (i + 2) % rows) for i in range(0, rows, 2)])
    near_l = lax.ppermute(left, "tx", flip)
    far_l = lax.ppermute(near_l, "tx", onward)
    crossing = jnp.where(odd, stepped, south_hi)
    crossing, _ = lax.optimization_barrier((crossing, far_p))
    hi_north = lax.ppermute(crossing, "tx", flip)
    probes_later, left_later, ebond, coeffs, _ = lax.optimization_barrier(
        (probes, left, ebond, coeffs, near_p)
    )
    coeffs = jnp.broadcast_to(coeffs[:, None], (coeffs.shape[0], orbs))
    east_edge = jnp.stack([probes_later[cols - 1], left_later[cols - 1]])
    west_edge = jnp.stack([probes_later[0], left_later[0]])
    edges = (lax.ppermute(east_edge, "ty", east), lax.ppermute(west_edge, "ty", west))
    last_bond = jnp.where(bond_mask[0, 0, cols - 1] != 0, ebond[cols - 1 :], 0).astype(BF16)
    east_in = lax.ppermute(last_bond, "ty", east)

    big = sds((cols, orbs, orbs), BF16)
    lanes = sds((cols, orbs), F32)

    def build(*refs):
        diag_kernel(*refs, scale=1.0 / count)

    diag, east_t, east_m, sine, cosine = call(
        build, (big, big, big, lanes, lanes),
        bond_mask[0, 0], hop, ebond, east_in, jnp.cos(angles), jnp.sin(angles), scalars=1,
    )
    near_m, far_m = call(
        vertical_kernel, (big, big), side, south_lo, south_hi, lo_even, lo_odd, hi_north, scalars=1
    )
    ops = (diag, east_t, east_m)
    part = [sds((2, width, count, orbs), F32) for width in widths]
    state = [sds((2, width, count, orbs), BF16) for width in widths]
    edge = sds((2, count, orbs), BF16)

    def across(k, parts, moved, first):
        def body(*refs):
            column_kernel(*refs, start=starts[k], first=first)

        shapes = (state[k], edge) if k in (0, chunks - 1) else (state[k],)
        return call(
            body, shapes, coeffs, near_m, far_m, parts[k], *moved, flops=2 * widths[k] * unit
        )

    def first_row(*refs):
        first_row_kernel(*refs, spots=spots)

    parts = call(
        first_row, part, coeffs, *ops, *edges, probes, left, flops=3 * cols * unit
    )
    made = {k: across(k, parts, (near_p, near_l, far_p, far_l), True) for k in order}
    states = []

    def row_parts(n, now, prev, edges):
        def body(*refs):
            row_kernel(*refs, spots=spots, level=3 - n, first=n == 1)

        return call(
            body, part, coeffs, *ops, *edges, left, *now, *prev, flops=3 * cols * unit
        )

    for n in (1, 2):
        now = [made[k][0] for k in range(chunks)]
        low, high = made[0][1], made[chunks - 1][1]
        states.append(now)
        near, far = [None] * chunks, [None] * chunks
        edges = (lax.ppermute(high, "ty", east), lax.ppermute(low, "ty", west))
        for j, k in enumerate(order):
            if j == 2:
                now[k], *edges = lax.optimization_barrier((now[k], *edges))
            near[k] = lax.ppermute(now[k], "tx", flip)
        prev = [probes] if n == 1 else states[-2]
        made = {}
        for j, k in enumerate(order):
            send = near[k]
            if j == chunks - 1:
                send, first, *more = lax.optimization_barrier((send, *made[order[0]]))
                made[order[0]] = [first, *more]
            far[k] = lax.ppermute(send, "tx", onward)
            if j == 0:
                parts = row_parts(n, now, prev, edges)
            if j >= chunks - 2:
                for i in order[: j + 1]:
                    if i not in made:
                        made[i] = across(i, parts, (near[i], far[i]), False)

    now = [made[k][0] for k in range(chunks)]
    low, high = made[0][1], made[chunks - 1][1]
    states.append(now)
    low, high = lax.optimization_barrier((low, high))
    edges = (lax.ppermute(high, "ty", east), lax.ppermute(low, "ty", west))
    sums = sds((2 * cols, orbs), F32)

    pieces = []
    for k in order:
        done = [starts[j] for j in order[:-1]] if k == order[-1] else []

        def far_sums(*refs, start=starts[k], done=done):
            far_kernel(*refs, start=start, done=done)

        shapes = (sums, sums) if done else (sds((4 * widths[k], orbs), F32),)
        pieces += call(
            far_sums, shapes, coeffs, near_m, far_m, near_p, far_p, near_l, far_l, now[k],
            *(pieces if done else []), flops=4 * widths[k] * unit,
        )
    to_partner, to_other = pieces[-2:]

    def near_sums(*refs):
        near_kernel(*refs, spots=spots)

    from_other = lax.ppermute(to_other, "tx", outer)
    from_partner = lax.ppermute(to_partner, "tx", flip)
    (own,) = call(
        near_sums, (sums,), coeffs, *ops, *edges, probes, left, *states[0], *states[1], *now,
        flops=6 * cols * unit,
    )
    (torque,) = call(
        torque_kernel, (sds((cols, orbs // 2), F32),),
        own, from_partner, from_other, sine, cosine,
    )
    return torque[None]


def solution(mesh):
    placed = (
        P("tx", "ty", None, None),
        P("tx", "ty", None, None),
        P("tx", "ty", None),
        P("tx", "ty", None, None),
        P("tx", "ty", None, None),
        P("tx", "ty", None, None),
        P(None, "tx", "ty"),
        P(),
    )
    return jax.shard_map(
        on_device, mesh=mesh, in_specs=placed, out_specs=P("tx", "ty", None), check_vma=False
    )
```

```python
import jax
import jax.numpy as jnp
from jax import lax
from jax.experimental import pallas as pl
from jax.experimental.pallas import tpu as pltpu
from jax.sharding import PartitionSpec as P

coupling = 0.5
SHARES = (4, 4, 4, 4)
F32 = jnp.float32
BF16 = jnp.bfloat16
VM = pl.BlockSpec(memory_space=pltpu.VMEM)
SM = pl.BlockSpec(memory_space=pltpu.SMEM)
HIGH = lax.Precision.HIGHEST


def mm(x, y):
    return lax.dot_general(x, y, (((1,), (0,)), ((), ())), preferred_element_type=F32)


def mm_t(x, y):
    return lax.dot_general(x, y, (((1,), (1,)), ((), ())), preferred_element_type=F32)


def sds(shape, dtype):
    return jax.ShapeDtypeStruct(tuple(shape), dtype)


def call(body, outs, *args, scalars=0, flops=0):
    nbytes = sum(a.size * a.dtype.itemsize for a in (*args, *outs))
    return pl.pallas_call(
        body,
        out_shape=tuple(outs),
        in_specs=[SM] * scalars + [VM] * (len(args) - scalars),
        out_specs=tuple(VM for _ in outs),
        cost_estimate=pl.CostEstimate(flops=flops, transcendentals=0, bytes_accessed=nbytes),
        compiler_params=pltpu.CompilerParams(vmem_limit_bytes=32 * 1024 * 1024),
    )(*args)


def lane_grid(rows, cols):
    return (
        lax.broadcasted_iota(jnp.int32, (rows, cols), 0),
        lax.broadcasted_iota(jnp.int32, (rows, cols), 1),
    )


def swap_matrix(orbs):
    row, col = lane_grid(orbs, orbs)
    return jnp.where(row == col + 1 - 2 * (col % 2), 1.0, 0.0).astype(BF16)


def scaled(coeff, value):
    return (coeff * value.astype(F32)).astype(BF16)


def places(widths):
    return [(k, i) for k, width in enumerate(widths) for i in range(width)]


def take(refs):
    def some(count):
        return [refs.pop(0) for _ in range(count)]

    return some


def diag_kernel(
    mask_ref, hop_ref, east_ref, edge_ref, cos_ref, sin_ref,
    diag_ref, east_t_ref, east_m_ref, signed_sin_ref, cos_out_ref, *, scale
):
    cols, orbs = hop_ref.shape[0], hop_ref.shape[1]
    site, lane = lane_grid(orbs // 2, orbs)
    spread = jnp.where(site == lane // 2, coupling, 0.0)
    signed = jnp.where(lane % 2 == 0, spread, -spread)
    cosine = jnp.dot(cos_ref[...], spread, precision=HIGH, preferred_element_type=F32)
    sine = jnp.dot(sin_ref[...], spread, precision=HIGH, preferred_element_type=F32)
    sign = jnp.where(lane[:1] % 2 == 0, 1.0, -1.0)
    signed_sin_ref[...] = scale * sign * sine
    cos_out_ref[...] = scale * cosine
    cosine = sign * cosine
    row, col = lane_grid(orbs, orbs)
    on_diag = row == col
    crossed = row == col + 1 - 2 * (col % 2)
    east_m_ref[0] = edge_ref[2:4].reshape(orbs, orbs)
    for c in range(cols):
        hop = hop_ref[c].astype(F32)
        onsite = jnp.where(on_diag, cosine[c : c + 1], 0.0)
        onsite = jnp.where(crossed, sine[c : c + 1], onsite)
        diag_ref[c] = (hop + hop.T + onsite).astype(BF16)
        east = east_ref[c].astype(F32) * mask_ref[c].astype(F32)
        east_t_ref[c] = east.T.astype(BF16)
        if c + 1 < cols:
            east_m_ref[c + 1] = east.astype(BF16)


def vertical_kernel(
    side_ref, own_lo, own_hi, lo_even, lo_odd, hi_north, partner_ref, other_ref
):
    half = own_lo.shape[0]

    def fill(south_out, north_out, lo_north):
        for begin, own_ref, north_ref in ((0, own_lo, lo_north), (half, own_hi, hi_north)):
            for c in range(half):
                south_out[begin + c] = own_ref[c].astype(F32).T.astype(BF16)
                north_out[begin + c] = north_ref[c]

    @pl.when(side_ref[0] == 0)
    def _():
        fill(partner_ref, other_ref, lo_even)

    @pl.when(side_ref[0] != 0)
    def _():
        fill(other_ref, partner_ref, lo_odd)


def both(ref, c):
    block = ref[:, c]
    return block.reshape(block.shape[0] * block.shape[1], block.shape[2])


def along_row(c, block, edge_refs, ops):
    diag_ref, east_t_ref, east_m_ref = ops
    cols = diag_ref.shape[0]

    def flat(ref):
        value = ref[...]
        return value.reshape(value.shape[0] * value.shape[1], value.shape[2])

    east = block(c + 1) if c + 1 < cols else flat(edge_refs[1])
    west = block(c - 1) if c > 0 else flat(edge_refs[0])
    total = mm(block(c), diag_ref[c])
    return total + mm(east, east_t_ref[c]) + mm(west, east_m_ref[c])


def first_row_kernel(coeff_ref, *refs, spots):
    some = take(list(refs))
    ops, edges, (probe_ref, left_ref) = some(3), some(2), some(2)
    outs = some(len(refs) - 7)
    cols, count = probe_ref.shape[0], probe_ref.shape[1]
    top = coeff_ref[coeff_ref.shape[0] - 1 :]

    def block(c):
        return jnp.concatenate([probe_ref[c], scaled(top, left_ref[c])], axis=0)

    edge_values = []
    for ref in edges:
        edge_values.append(jnp.concatenate([ref[0], scaled(top, ref[1])], axis=0)[None])
    blocks = [block(c) for c in range(cols)]
    for c in range(cols):
        total = along_row(c, lambda i: blocks[i], edge_values, ops)
        base = coeff_ref[3:4] * left_ref[c].astype(F32)
        k, i = spots[c]
        outs[k][0, i] = total[:count]
        outs[k][1, i] = 2.0 * total[count:] + base


def row_kernel(coeff_ref, *refs, spots, level, first):
    some = take(list(refs))
    ops, edges, (left_ref,) = some(3), some(2), some(1)
    cols = left_ref.shape[0]
    chunks = spots[-1][0] + 1
    states = some(chunks)
    prevs = some(1) if first else some(chunks)
    outs = some(chunks)
    count = left_ref.shape[1]

    def block(c):
        return both(states[spots[c][0]], spots[c][1])

    for c in range(cols):
        k, i = spots[c]
        total = 2.0 * along_row(c, block, edges, ops)
        if first:
            old_a = prevs[0][c]
            old_g = scaled(coeff_ref[coeff_ref.shape[0] - 1 :], left_ref[c])
        else:
            old_a, old_g = prevs[k][0, i], prevs[k][1, i]
        base = coeff_ref[level : level + 1] * left_ref[c].astype(F32)
        outs[k][0, i] = total[:count] - old_a.astype(F32)
        outs[k][1, i] = total[count:] + base - old_g.astype(F32)


def column_kernel(coeff_ref, *refs, start, first):
    some = take(list(refs))
    ops, (part_ref,) = some(2), some(1)
    moved = some(4 if first else 2)
    out_ref, *edge = some(len(refs) - 3 - len(moved))
    width, count = part_ref.shape[1], part_ref.shape[2]
    top = coeff_ref[coeff_ref.shape[0] - 1 :]
    for i in range(width):
        c = start + i
        if first:
            near, far = [
                jnp.concatenate([a[c], scaled(top, g[c])], axis=0)
                for a, g in (moved[:2], moved[2:])
            ]
        else:
            near, far = both(moved[0], i), both(moved[1], i)
        total = mm(near, ops[0][c]) + mm(far, ops[1][c])
        factor = 1.0 if first else 2.0
        new_a = (part_ref[0, i] + factor * total[:count]).astype(BF16)
        new_g = (part_ref[1, i] + 2.0 * total[count:]).astype(BF16)
        out_ref[0, i] = new_a
        out_ref[1, i] = new_g
        if edge and i == (0 if start == 0 else width - 1):
            edge[0][0] = new_a
            edge[0][1] = new_g


def far_kernel(coeff_ref, *refs, start, done):
    some = take(list(refs))
    ops, probe_refs, left_refs, (state_ref,) = some(2), some(2), some(2), some(1)
    earlier = some(len(done))
    out_refs = some(1 if not done else 2)
    cols, _, orbs = probe_refs[0].shape
    width, count = state_ref.shape[1], state_ref.shape[2]
    top = coeff_ref[coeff_ref.shape[0] - 1 :]
    swap = swap_matrix(orbs)
    for side in range(2):
        for i in range(width):
            c = start + i
            moved = mm_t(both(state_ref, i), ops[side][c])
            moved_a, moved_g = 4.0 * moved[:count], 2.0 * moved[count:]
            p, left = probe_refs[side][c], scaled(top, left_refs[side][c])
            same = moved_g * p.astype(F32) + moved_a * left.astype(F32)
            cross = moved_g * mm(p, swap) + moved_a * mm(left, swap)
            for row, value in ((0, same), (1, cross)):
                value = jnp.sum(value, axis=0, keepdims=True)
                if done:
                    out_refs[side][row * cols + c : row * cols + c + 1, :] = value
                else:
                    at = (2 * side + row) * width + i
                    out_refs[0][at : at + 1, :] = value
        for ref, begin in zip(earlier, done):
            size = ref.shape[0] // 4
            for row in range(2):
                at = (2 * side + row) * size
                to = row * cols + begin
                out_refs[side][to : to + size, :] = ref[at : at + size, :]


def near_kernel(coeff_ref, *refs, spots):
    some = take(list(refs))
    ops, edges, (probe_ref, left_ref) = some(3), some(2), some(2)
    cols, count, orbs = probe_ref.shape
    chunks = spots[-1][0] + 1
    first, second, third = some(chunks), some(chunks), some(chunks)
    (out_ref,) = some(1)
    top = coeff_ref[coeff_ref.shape[0] - 1 :]
    swap = swap_matrix(orbs)

    def block(c):
        return both(third[spots[c][0]], spots[c][1])

    for c in range(cols):
        k, i = spots[c]
        a = [probe_ref[c], first[k][0, i], second[k][0, i], third[k][0, i]]
        g = [third[k][1, i], second[k][1, i], first[k][1, i], scaled(top, left_ref[c])]
        total = 2.0 * along_row(c, block, edges, ops)
        last_a = total[:count] - a[2].astype(F32)
        last_g = total[count:] + coeff_ref[:1] * left_ref[c].astype(F32) - g[1].astype(F32)
        same = last_g * a[0].astype(F32)
        cross = last_g * mm(a[0], swap)
        same2 = last_a * g[3].astype(F32)
        cross2 = last_a * mm(g[3], swap)
        for n in range(3):
            same2 = same2 + g[n].astype(F32) * a[n + 1].astype(F32)
            cross2 = cross2 + g[n].astype(F32) * mm(a[n + 1], swap)
        out_ref[c : c + 1, :] = jnp.sum(same + 2.0 * same2, axis=0, keepdims=True)
        out_ref[cols + c : cols + c + 1, :] = jnp.sum(cross + 2.0 * cross2, axis=0, keepdims=True)


def torque_kernel(near_ref, partner_ref, other_ref, sin_ref, cos_ref, out_ref):
    total = near_ref[...] + partner_ref[...] + other_ref[...]
    cols, orbs = total.shape[0] // 2, total.shape[1]
    lane, site = lane_grid(orbs, orbs // 2)
    gather = jnp.where(lane // 2 == site, 1.0, 0.0)
    lanes = sin_ref[...] * total[:cols] - cos_ref[...] * total[cols:]
    out_ref[...] = jnp.dot(lanes, gather, precision=HIGH, preferred_element_type=F32)


def on_device(
    probes, left_probes, angles, cluster_hopping, east_bonds, south_bonds, bond_mask, coeffs
):
    rows, columns = (lax.axis_size("tx"), lax.axis_size("ty"))
    flip = [(i, i ^ 1) for i in range(rows)]
    onward = [(i, (i + 2) % rows if i % 2 == 0 else (i - 2) % rows) for i in range(rows)]
    outer = [(i, (i - 1) % rows if i % 2 == 0 else (i + 1) % rows) for i in range(rows)]
    south = [(i, (i + 1) % rows) for i in range(rows)]
    east = [(i, (i + 1) % columns) for i in range(columns)]
    west = [(j, i) for i, j in east]
    side = (lax.axis_index("tx") % 2).astype(jnp.int32).reshape(1)

    probes, left, angles = probes[0], left_probes[0], angles[0]
    hop, ebond, sbond = cluster_hopping[0], east_bonds[0], south_bonds[0]
    cols, count, orbs = probes.shape
    widths = [cols * part // 16 for part in SHARES]
    chunks = len(widths)
    starts = [sum(widths[:k]) for k in range(chunks)]
    spots = places(widths)
    order = [0, chunks - 1, *range(1, chunks - 1)]
    unit = 4 * count * orbs * orbs
    half = cols // 2

    odd = lax.axis_index("tx") % 2 == 1
    near_p = lax.ppermute(probes, "tx", flip)
    far_p = lax.ppermute(near_p, "tx", onward)
    present = bond_mask[1, 0][:, None, None] != 0
    south_lo, south_hi = [
        jnp.where(present[part], sbond[part], jnp.zeros_like(sbond[part]))
        for part in (slice(0, half), slice(half, cols))
    ]
    stepped = lax.ppermute(south_hi, "tx", [(i, (i + 2) % rows) for i in range(1, rows, 2)])
    lo_odd = lax.ppermute(south_lo, "tx", flip)
    lo_even = lax.ppermute(lo_odd, "tx", [(i, (i + 2) % rows) for i in range(0, rows, 2)])
    near_l = lax.ppermute(left, "tx", flip)
    far_l = lax.ppermute(near_l, "tx", onward)
    crossing = jnp.where(odd, stepped, south_hi)
    crossing, _ = lax.optimization_barrier((crossing, far_p))
    hi_north = lax.ppermute(crossing, "tx", flip)
    probes_later, left_later, ebond, coeffs, _ = lax.optimization_barrier(
        (probes, left, ebond, coeffs, near_p)
    )
    coeffs = jnp.broadcast_to(coeffs[:, None], (coeffs.shape[0], orbs))
    last_bond = jnp.where(bond_mask[0, 0, cols - 1] != 0, ebond[cols - 1], 0).astype(BF16)
    east_edge = jnp.concatenate(
        [probes_later[cols - 1 :], left_later[cols - 1 :], last_bond.reshape(2, count, orbs)]
    )
    west_edge = jnp.stack([probes_later[0], left_later[0]])
    edges = (lax.ppermute(east_edge, "ty", east), lax.ppermute(west_edge, "ty", west))

    big = sds((cols, orbs, orbs), BF16)
    lanes = sds((cols, orbs), F32)

    def build(*refs):
        diag_kernel(*refs, scale=1.0 / count)

    diag, east_t, east_m, sine, cosine = call(
        build, (big, big, big, lanes, lanes),
        bond_mask[0, 0], hop, ebond, edges[0], jnp.cos(angles), jnp.sin(angles), scalars=1,
    )
    near_m, far_m = call(
        vertical_kernel, (big, big), side, south_lo, south_hi, lo_even, lo_odd, hi_north, scalars=1
    )
    ops = (diag, east_t, east_m)
    part = [sds((2, width, count, orbs), F32) for width in widths]
    state = [sds((2, width, count, orbs), BF16) for width in widths]
    edge = sds((2, count, orbs), BF16)

    def across(k, parts, moved, first):
        def body(*refs):
            column_kernel(*refs, start=starts[k], first=first)

        shapes = (state[k], edge) if k in (0, chunks - 1) else (state[k],)
        return call(
            body, shapes, coeffs, near_m, far_m, parts[k], *moved, flops=2 * widths[k] * unit
        )

    def first_row(*refs):
        first_row_kernel(*refs, spots=spots)

    parts = call(
        first_row, part, coeffs, *ops, *edges, probes, left, flops=3 * cols * unit
    )
    made = {k: across(k, parts, (near_p, near_l, far_p, far_l), True) for k in order}
    states = []

    def row_parts(n, now, prev, edges):
        def body(*refs):
            row_kernel(*refs, spots=spots, level=3 - n, first=n == 1)

        return call(
            body, part, coeffs, *ops, *edges, left, *now, *prev, flops=3 * cols * unit
        )

    for n in (1, 2):
        now = [made[k][0] for k in range(chunks)]
        low, high = made[0][1], made[chunks - 1][1]
        states.append(now)
        near, far = [None] * chunks, [None] * chunks
        edges = (lax.ppermute(high, "ty", east), lax.ppermute(low, "ty", west))
        for j, k in enumerate(order):
            if j == 2:
                now[k], *edges = lax.optimization_barrier((now[k], *edges))
            near[k] = lax.ppermute(now[k], "tx", flip)
        prev = [probes] if n == 1 else states[-2]
        made = {}
        for j, k in enumerate(order):
            send = near[k]
            if j == chunks - 1:
                send, first, *more = lax.optimization_barrier((send, *made[order[0]]))
                made[order[0]] = [first, *more]
            far[k] = lax.ppermute(send, "tx", onward)
            if j == 0:
                parts = row_parts(n, now, prev, edges)
            if j >= chunks - 2:
                for i in order[: j + 1]:
                    if i not in made:
                        made[i] = across(i, parts, (near[i], far[i]), False)

    now = [made[k][0] for k in range(chunks)]
    low, high = made[0][1], made[chunks - 1][1]
    states.append(now)
    low, high = lax.optimization_barrier((low, high))
    edges = (lax.ppermute(high, "ty", east), lax.ppermute(low, "ty", west))
    sums = sds((2 * cols, orbs), F32)

    pieces = []
    for k in order:
        done = [starts[j] for j in order[:-1]] if k == order[-1] else []

        def far_sums(*refs, start=starts[k], done=done):
            far_kernel(*refs, start=start, done=done)

        shapes = (sums, sums) if done else (sds((4 * widths[k], orbs), F32),)
        pieces += call(
            far_sums, shapes, coeffs, near_m, far_m, near_p, far_p, near_l, far_l, now[k],
            *(pieces if done else []), flops=4 * widths[k] * unit,
        )
    to_partner, to_other = pieces[-2:]

    def near_sums(*refs):
        near_kernel(*refs, spots=spots)

    to_other, to_partner, *edges = lax.optimization_barrier((to_other, to_partner, *edges))
    from_other = lax.ppermute(to_other, "tx", outer)
    from_partner = lax.ppermute(to_partner, "tx", flip)
    (own,) = call(
        near_sums, (sums,), coeffs, *ops, *edges, probes, left, *states[0], *states[1], *now,
        flops=6 * cols * unit,
    )
    (torque,) = call(
        torque_kernel, (sds((cols, orbs // 2), F32),),
        own, from_partner, from_other, sine, cosine,
    )
    return torque[None]


def solution(mesh):
    placed = (
        P("tx", "ty", None, None),
        P("tx", "ty", None, None),
        P("tx", "ty", None),
        P("tx", "ty", None, None),
        P("tx", "ty", None, None),
        P("tx", "ty", None, None),
        P(None, "tx", "ty"),
        P(),
    )
    return jax.shard_map(
        on_device, mesh=mesh, in_specs=placed, out_specs=P("tx", "ty", None), check_vma=False
    )
```

```python
import jax
import jax.numpy as jnp
from jax import lax
from jax.experimental import pallas as pl
from jax.experimental.pallas import tpu as pltpu
from jax.sharding import PartitionSpec as P

coupling = 0.5
SHARES = (4, 4, 4, 4)
F32 = jnp.float32
BF16 = jnp.bfloat16
VM = pl.BlockSpec(memory_space=pltpu.VMEM)
SM = pl.BlockSpec(memory_space=pltpu.SMEM)
HIGH = lax.Precision.HIGHEST


def mm(x, y):
    return lax.dot_general(x, y, (((1,), (0,)), ((), ())), preferred_element_type=F32)


def mm_t(x, y):
    return lax.dot_general(x, y, (((1,), (1,)), ((), ())), preferred_element_type=F32)


def sds(shape, dtype):
    return jax.ShapeDtypeStruct(tuple(shape), dtype)


def call(body, outs, *args, scalars=0, flops=0):
    nbytes = sum(a.size * a.dtype.itemsize for a in (*args, *outs))
    return pl.pallas_call(
        body,
        out_shape=tuple(outs),
        in_specs=[SM] * scalars + [VM] * (len(args) - scalars),
        out_specs=tuple(VM for _ in outs),
        cost_estimate=pl.CostEstimate(flops=flops, transcendentals=0, bytes_accessed=nbytes),
        compiler_params=pltpu.CompilerParams(vmem_limit_bytes=32 * 1024 * 1024),
    )(*args)


def lane_grid(rows, cols):
    return (
        lax.broadcasted_iota(jnp.int32, (rows, cols), 0),
        lax.broadcasted_iota(jnp.int32, (rows, cols), 1),
    )


def swap_matrix(orbs):
    row, col = lane_grid(orbs, orbs)
    return jnp.where(row == col + 1 - 2 * (col % 2), 1.0, 0.0).astype(BF16)


def scaled(coeff, value):
    return (coeff * value.astype(F32)).astype(BF16)


def places(widths):
    return [(k, i) for k, width in enumerate(widths) for i in range(width)]


def take(refs):
    def some(count):
        return [refs.pop(0) for _ in range(count)]

    return some


def diag_kernel(
    mask_ref, hop_ref, east_ref, edge_ref, cos_ref, sin_ref,
    diag_ref, east_t_ref, east_m_ref, signed_sin_ref, cos_out_ref, *, scale
):
    cols, orbs = hop_ref.shape[0], hop_ref.shape[1]
    site, lane = lane_grid(orbs // 2, orbs)
    spread = jnp.where(site == lane // 2, coupling, 0.0)
    signed = jnp.where(lane % 2 == 0, spread, -spread)
    cosine = jnp.dot(cos_ref[...], spread, precision=HIGH, preferred_element_type=F32)
    sine = jnp.dot(sin_ref[...], spread, precision=HIGH, preferred_element_type=F32)
    sign = jnp.where(lane[:1] % 2 == 0, 1.0, -1.0)
    signed_sin_ref[...] = scale * sign * sine
    cos_out_ref[...] = scale * cosine
    cosine = sign * cosine
    row, col = lane_grid(orbs, orbs)
    on_diag = row == col
    crossed = row == col + 1 - 2 * (col % 2)
    east_m_ref[0] = edge_ref[2:4].reshape(orbs, orbs)
    for c in range(cols):
        hop = hop_ref[c].astype(F32)
        onsite = jnp.where(on_diag, cosine[c : c + 1], 0.0)
        onsite = jnp.where(crossed, sine[c : c + 1], onsite)
        diag_ref[c] = (hop + hop.T + onsite).astype(BF16)
        east = east_ref[c].astype(F32) * mask_ref[c].astype(F32)
        east_t_ref[c] = east.T.astype(BF16)
        if c + 1 < cols:
            east_m_ref[c + 1] = east.astype(BF16)


def vertical_kernel(
    side_ref, own_lo, own_hi, lo_even, lo_odd, hi_north, partner_ref, other_ref
):
    half = own_lo.shape[0]

    def fill(south_out, north_out, lo_north):
        for begin, own_ref, north_ref in ((0, own_lo, lo_north), (half, own_hi, hi_north)):
            for c in range(half):
                south_out[begin + c] = own_ref[c].astype(F32).T.astype(BF16)
                north_out[begin + c] = north_ref[c]

    @pl.when(side_ref[0] == 0)
    def _():
        fill(partner_ref, other_ref, lo_even)

    @pl.when(side_ref[0] != 0)
    def _():
        fill(other_ref, partner_ref, lo_odd)


def both(ref, c):
    block = ref[:, c]
    return block.reshape(block.shape[0] * block.shape[1], block.shape[2])


def along_row(c, block, edge_refs, ops):
    diag_ref, east_t_ref, east_m_ref = ops
    cols = diag_ref.shape[0]

    def flat(ref):
        value = ref[...]
        return value.reshape(value.shape[0] * value.shape[1], value.shape[2])

    east = block(c + 1) if c + 1 < cols else flat(edge_refs[1])
    west = block(c - 1) if c > 0 else flat(edge_refs[0])
    total = mm(block(c), diag_ref[c])
    return total + mm(east, east_t_ref[c]) + mm(west, east_m_ref[c])


def first_row_kernel(coeff_ref, *refs, spots):
    some = take(list(refs))
    ops, edges, (probe_ref, left_ref) = some(3), some(2), some(2)
    outs = some(len(refs) - 7)
    cols, count = probe_ref.shape[0], probe_ref.shape[1]
    top = coeff_ref[coeff_ref.shape[0] - 1 :]

    def block(c):
        return jnp.concatenate([probe_ref[c], scaled(top, left_ref[c])], axis=0)

    edge_values = []
    for ref in edges:
        edge_values.append(jnp.concatenate([ref[0], scaled(top, ref[1])], axis=0)[None])
    blocks = [block(c) for c in range(cols)]
    for c in range(cols):
        total = along_row(c, lambda i: blocks[i], edge_values, ops)
        base = coeff_ref[3:4] * left_ref[c].astype(F32)
        k, i = spots[c]
        outs[k][0, i] = total[:count]
        outs[k][1, i] = 2.0 * total[count:] + base


def row_kernel(coeff_ref, *refs, spots, level, first):
    some = take(list(refs))
    ops, edges, (left_ref,) = some(3), some(2), some(1)
    cols = left_ref.shape[0]
    chunks = spots[-1][0] + 1
    states = some(chunks)
    prevs = some(1) if first else some(chunks)
    outs = some(chunks)
    count = left_ref.shape[1]

    def block(c):
        return both(states[spots[c][0]], spots[c][1])

    for c in range(cols):
        k, i = spots[c]
        total = 2.0 * along_row(c, block, edges, ops)
        if first:
            old_a = prevs[0][c]
            old_g = scaled(coeff_ref[coeff_ref.shape[0] - 1 :], left_ref[c])
        else:
            old_a, old_g = prevs[k][0, i], prevs[k][1, i]
        base = coeff_ref[level : level + 1] * left_ref[c].astype(F32)
        outs[k][0, i] = total[:count] - old_a.astype(F32)
        outs[k][1, i] = total[count:] + base - old_g.astype(F32)


def column_kernel(coeff_ref, *refs, start, first):
    some = take(list(refs))
    ops, (part_ref,) = some(2), some(1)
    moved = some(4 if first else 2)
    out_ref, *edge = some(len(refs) - 3 - len(moved))
    width, count = part_ref.shape[1], part_ref.shape[2]
    top = coeff_ref[coeff_ref.shape[0] - 1 :]
    for i in range(width):
        c = start + i
        if first:
            near, far = [
                jnp.concatenate([a[c], scaled(top, g[c])], axis=0)
                for a, g in (moved[:2], moved[2:])
            ]
        else:
            near, far = both(moved[0], i), both(moved[1], i)
        total = mm(near, ops[0][c]) + mm(far, ops[1][c])
        factor = 1.0 if first else 2.0
        new_a = (part_ref[0, i] + factor * total[:count]).astype(BF16)
        new_g = (part_ref[1, i] + 2.0 * total[count:]).astype(BF16)
        out_ref[0, i] = new_a
        out_ref[1, i] = new_g
        if edge and i == (0 if start == 0 else width - 1):
            edge[0][0] = new_a
            edge[0][1] = new_g


def far_kernel(coeff_ref, *refs, start, done):
    some = take(list(refs))
    ops, probe_refs, left_refs, (state_ref,) = some(2), some(2), some(2), some(1)
    earlier = some(len(done))
    out_refs = some(1 if not done else 2)
    cols, _, orbs = probe_refs[0].shape
    width, count = state_ref.shape[1], state_ref.shape[2]
    top = coeff_ref[coeff_ref.shape[0] - 1 :]
    swap = swap_matrix(orbs)
    for side in range(2):
        for i in range(width):
            c = start + i
            moved = mm_t(both(state_ref, i), ops[side][c])
            moved_a, moved_g = 4.0 * moved[:count], 2.0 * moved[count:]
            p, left = probe_refs[side][c], scaled(top, left_refs[side][c])
            same = moved_g * p.astype(F32) + moved_a * left.astype(F32)
            cross = moved_g * mm(p, swap) + moved_a * mm(left, swap)
            for row, value in ((0, same), (1, cross)):
                value = jnp.sum(value, axis=0, keepdims=True)
                if done:
                    out_refs[side][row * cols + c : row * cols + c + 1, :] = value
                else:
                    at = (2 * side + row) * width + i
                    out_refs[0][at : at + 1, :] = value
        for ref, begin in zip(earlier, done):
            size = ref.shape[0] // 4
            for row in range(2):
                at = (2 * side + row) * size
                to = row * cols + begin
                out_refs[side][to : to + size, :] = ref[at : at + size, :]


def near_kernel(coeff_ref, *refs, spots):
    some = take(list(refs))
    ops, edges, (probe_ref, left_ref) = some(3), some(2), some(2)
    cols, count, orbs = probe_ref.shape
    chunks = spots[-1][0] + 1
    first, second, third = some(chunks), some(chunks), some(chunks)
    (out_ref,) = some(1)
    top = coeff_ref[coeff_ref.shape[0] - 1 :]
    swap = swap_matrix(orbs)

    def block(c):
        return both(third[spots[c][0]], spots[c][1])

    for c in range(cols):
        k, i = spots[c]
        a = [probe_ref[c], first[k][0, i], second[k][0, i], third[k][0, i]]
        g = [third[k][1, i], second[k][1, i], first[k][1, i], scaled(top, left_ref[c])]
        total = 2.0 * along_row(c, block, edges, ops)
        last_a = total[:count] - a[2].astype(F32)
        last_g = total[count:] + coeff_ref[:1] * left_ref[c].astype(F32) - g[1].astype(F32)
        same = last_g * a[0].astype(F32)
        cross = last_g * mm(a[0], swap)
        same2 = last_a * g[3].astype(F32)
        cross2 = last_a * mm(g[3], swap)
        for n in range(3):
            same2 = same2 + g[n].astype(F32) * a[n + 1].astype(F32)
            cross2 = cross2 + g[n].astype(F32) * mm(a[n + 1], swap)
        out_ref[c : c + 1, :] = jnp.sum(same + 2.0 * same2, axis=0, keepdims=True)
        out_ref[cols + c : cols + c + 1, :] = jnp.sum(cross + 2.0 * cross2, axis=0, keepdims=True)


def torque_kernel(near_ref, partner_ref, other_ref, sin_ref, cos_ref, out_ref):
    total = near_ref[...] + partner_ref[...] + other_ref[...]
    cols, orbs = total.shape[0] // 2, total.shape[1]
    lane, site = lane_grid(orbs, orbs // 2)
    gather = jnp.where(lane // 2 == site, 1.0, 0.0)
    lanes = sin_ref[...] * total[:cols] - cos_ref[...] * total[cols:]
    out_ref[...] = jnp.dot(lanes, gather, precision=HIGH, preferred_element_type=F32)


def on_device(
    probes, left_probes, angles, cluster_hopping, east_bonds, south_bonds, bond_mask, coeffs
):
    rows, columns = (lax.axis_size("tx"), lax.axis_size("ty"))
    flip = [(i, i ^ 1) for i in range(rows)]
    onward = [(i, (i + 2) % rows if i % 2 == 0 else (i - 2) % rows) for i in range(rows)]
    outer = [(i, (i - 1) % rows if i % 2 == 0 else (i + 1) % rows) for i in range(rows)]
    south = [(i, (i + 1) % rows) for i in range(rows)]
    east = [(i, (i + 1) % columns) for i in range(columns)]
    west = [(j, i) for i, j in east]
    side = (lax.axis_index("tx") % 2).astype(jnp.int32).reshape(1)

    probes, left, angles = probes[0], left_probes[0], angles[0]
    hop, ebond, sbond = cluster_hopping[0], east_bonds[0], south_bonds[0]
    cols, count, orbs = probes.shape
    widths = [cols * part // 16 for part in SHARES]
    chunks = len(widths)
    starts = [sum(widths[:k]) for k in range(chunks)]
    spots = places(widths)
    order = [0, chunks - 1, *range(1, chunks - 1)]
    unit = 4 * count * orbs * orbs
    half = cols // 2

    odd = lax.axis_index("tx") % 2 == 1
    near_p = lax.ppermute(probes, "tx", flip)
    far_p = lax.ppermute(near_p, "tx", onward)
    present = bond_mask[1, 0][:, None, None] != 0
    south_lo, south_hi = [
        jnp.where(present[part], sbond[part], jnp.zeros_like(sbond[part]))
        for part in (slice(0, half), slice(half, cols))
    ]
    stepped = lax.ppermute(south_hi, "tx", [(i, (i + 2) % rows) for i in range(1, rows, 2)])
    lo_odd = lax.ppermute(south_lo, "tx", flip)
    lo_even = lax.ppermute(lo_odd, "tx", [(i, (i + 2) % rows) for i in range(0, rows, 2)])
    left_send, _ = lax.optimization_barrier((left, south_lo))
    near_l = lax.ppermute(left_send, "tx", flip)
    far_l = lax.ppermute(near_l, "tx", onward)
    crossing = jnp.where(odd, stepped, south_hi)
    crossing, _ = lax.optimization_barrier((crossing, far_p))
    hi_north = lax.ppermute(crossing, "tx", flip)
    probes_later, left_later, ebond, coeffs, _ = lax.optimization_barrier(
        (probes, left, ebond, coeffs, near_p)
    )
    coeffs = jnp.broadcast_to(coeffs[:, None], (coeffs.shape[0], orbs))
    last_bond = jnp.where(bond_mask[0, 0, cols - 1] != 0, ebond[cols - 1], 0).astype(BF16)
    east_edge = jnp.concatenate(
        [probes_later[cols - 1 :], left_later[cols - 1 :], last_bond.reshape(2, count, orbs)]
    )
    west_edge = jnp.stack([probes_later[0], left_later[0]])
    edges = (lax.ppermute(east_edge, "ty", east), lax.ppermute(west_edge, "ty", west))

    big = sds((cols, orbs, orbs), BF16)
    lanes = sds((cols, orbs), F32)

    def build(*refs):
        diag_kernel(*refs, scale=1.0 / count)

    diag, east_t, east_m, sine, cosine = call(
        build, (big, big, big, lanes, lanes),
        bond_mask[0, 0], hop, ebond, edges[0], jnp.cos(angles), jnp.sin(angles), scalars=1,
    )
    near_m, far_m = call(
        vertical_kernel, (big, big), side, south_lo, south_hi, lo_even, lo_odd, hi_north, scalars=1
    )
    ops = (diag, east_t, east_m)
    part = [sds((2, width, count, orbs), F32) for width in widths]
    state = [sds((2, width, count, orbs), BF16) for width in widths]
    edge = sds((2, count, orbs), BF16)

    def across(k, parts, moved, first):
        def body(*refs):
            column_kernel(*refs, start=starts[k], first=first)

        shapes = (state[k], edge) if k in (0, chunks - 1) else (state[k],)
        return call(
            body, shapes, coeffs, near_m, far_m, parts[k], *moved, flops=2 * widths[k] * unit
        )

    def first_row(*refs):
        first_row_kernel(*refs, spots=spots)

    parts = call(
        first_row, part, coeffs, *ops, *edges, probes, left, flops=3 * cols * unit
    )
    made = {k: across(k, parts, (near_p, near_l, far_p, far_l), True) for k in order}
    states = []

    def row_parts(n, now, prev, edges):
        def body(*refs):
            row_kernel(*refs, spots=spots, level=3 - n, first=n == 1)

        return call(
            body, part, coeffs, *ops, *edges, left, *now, *prev, flops=3 * cols * unit
        )

    for n in (1, 2):
        now = [made[k][0] for k in range(chunks)]
        low, high = made[0][1], made[chunks - 1][1]
        states.append(now)
        near, far = [None] * chunks, [None] * chunks
        edges = (lax.ppermute(high, "ty", east), lax.ppermute(low, "ty", west))
        for j, k in enumerate(order):
            if j == 2:
                now[k], *edges = lax.optimization_barrier((now[k], *edges))
            near[k] = lax.ppermute(now[k], "tx", flip)
        prev = [probes] if n == 1 else states[-2]
        made = {}
        for j, k in enumerate(order):
            send = near[k]
            if j == chunks - 1:
                send, first, *more = lax.optimization_barrier((send, *made[order[0]]))
                made[order[0]] = [first, *more]
            far[k] = lax.ppermute(send, "tx", onward)
            if j == 0:
                parts = row_parts(n, now, prev, edges)
            if j >= chunks - 2:
                for i in order[: j + 1]:
                    if i not in made:
                        made[i] = across(i, parts, (near[i], far[i]), False)

    now = [made[k][0] for k in range(chunks)]
    low, high = made[0][1], made[chunks - 1][1]
    states.append(now)
    low, high = lax.optimization_barrier((low, high))
    edges = (lax.ppermute(high, "ty", east), lax.ppermute(low, "ty", west))
    sums = sds((2 * cols, orbs), F32)

    pieces = []
    for k in order:
        done = [starts[j] for j in order[:-1]] if k == order[-1] else []

        def far_sums(*refs, start=starts[k], done=done):
            far_kernel(*refs, start=start, done=done)

        shapes = (sums, sums) if done else (sds((4 * widths[k], orbs), F32),)
        pieces += call(
            far_sums, shapes, coeffs, near_m, far_m, near_p, far_p, near_l, far_l, now[k],
            *(pieces if done else []), flops=4 * widths[k] * unit,
        )
    to_partner, to_other = pieces[-2:]

    def near_sums(*refs):
        near_kernel(*refs, spots=spots)

    to_other, to_partner, *edges = lax.optimization_barrier((to_other, to_partner, *edges))
    from_other = lax.ppermute(to_other, "tx", outer)
    from_partner = lax.ppermute(to_partner, "tx", flip)
    (own,) = call(
        near_sums, (sums,), coeffs, *ops, *edges, probes, left, *states[0], *states[1], *now,
        flops=6 * cols * unit,
    )
    (torque,) = call(
        torque_kernel, (sds((cols, orbs // 2), F32),),
        own, from_partner, from_other, sine, cosine,
    )
    return torque[None]


def solution(mesh):
    placed = (
        P("tx", "ty", None, None),
        P("tx", "ty", None, None),
        P("tx", "ty", None),
        P("tx", "ty", None, None),
        P("tx", "ty", None, None),
        P("tx", "ty", None, None),
        P(None, "tx", "ty"),
        P(),
    )
    return jax.shard_map(
        on_device, mesh=mesh, in_specs=placed, out_specs=P("tx", "ty", None), check_vma=False
    )
```
